32 devices in a mesh: wide: 8 (over z, y), narrow: 4 (over x, core).
Axes of the slice: x: 2, y: 2, z: 4, core: 2. Of those that a mesh axis runs over, the one named last changes fastest.
Arguments:
- charges: bfloat16 [4, 192, 64, 64], P('narrow', 'wide'), may hold values from -6 to 6
- leaf_row_basis: bfloat16 [4, 192, 64, 64], P('narrow', 'wide'), may hold values from -0.75 to 0.75
- leaf_column_basis: bfloat16 [4, 192, 64, 64], P('narrow', 'wide'), may hold values from -0.75 to 0.75
- near_blocks: bfloat16 [4, 192, 8, 64, 64], P('narrow', 'wide'), may hold values from -0.75 to 0.75
- near_src: int32 [4, 192, 8], P('narrow', 'wide'), may hold values from 0 to 191, as said below
- near_count: int32 [4, 192], P('narrow', 'wide'), may hold values from 2 to 8, as said below
- leaf_coupling: bfloat16 [4, 192, 6, 64, 64], P('narrow', 'wide'), may hold values from -0.75 to 0.75
- far_src: int32 [4, 192, 6], P('narrow', 'wide'), may hold values from 0 to 191, as said below
- up_leaf: bfloat16 [4, 192, 64, 64], P('narrow', 'wide'), may hold values from -0.375 to 0.375
- column_transfer_leaf: bfloat16 [4, 192, 64, 64], P('narrow', 'wide'), may hold values from -0.75 to 0.75
- mid_coupling: bfloat16 [4, 48, 6, 64, 64], P('narrow', 'wide'), may hold values from -0.75 to 0.75
- mid_src: int32 [4, 48, 6], P('narrow', 'wide'), may hold values from 0 to 47, as said below
- up_mid: bfloat16 [4, 48, 64, 64], P('narrow', 'wide'), may hold values from -0.3125 to 0.3125
- down_mid: bfloat16 [4, 48, 64, 64], P('narrow', 'wide'), may hold values from -0.75 to 0.75
- up_top: bfloat16 [4, 8, 64, 64], P('narrow', 'wide'), may hold values from -0.25 to 0.25
- down_top: bfloat16 [4, 8, 64, 64], P('narrow', 'wide'), may hold values from -0.75 to 0.75
- top_coupling: bfloat16 [4, 4, 64, 64], P('narrow'), may hold values from -0.75 to 0.75
Outputs:
- sensitivity: bfloat16 [4, 192, 64, 64], P('narrow', 'wide')
The draws below stay inside these ranges and needn't reach their ends.
Inputs may be any that keep to these rules, and one draw needn't show every extreme that they name: near_src[g, i, 0] is i itself, and every entry differs from i by at most 8; some entry differs by exactly 8. Leaf i uses the first near_count[g, i] slots of its near-field list. `far_src`: every entry differs from its leaf i by 2 to 8. `mid_src`: every entry differs from its mid-level cluster m by 2 to 6.
All inputs are finite; a program needn't handle non-finite values.
Results may differ from the reference program's by a relative error of at most 0.009.
Values may be sent and summed in bfloat16 or wider, within the bound.
No kernel may reach another device: no remote copies, remote signals or barrier semaphores. Data moves between devices by JAX's collectives and lax.ppermute only.
A program may use at most 64 MiB of HBM per device.

```python
import jax
import jax.numpy as jnp
from jax import lax

LEAF = 64
RANK = 64
RHS = 64
NEAR_MAX = 8
FAR = 6
MFAR = 6
REACH = 8
MD = 6
GROUPS = 4
GLEAVES = 192
GMIDS = 48
N_WIDE = 8


def near_lists(key):
    base = jax.random.fold_in(key, 11)
    key_off, key_count = jax.random.split(base, 2)
    index = jnp.arange(GLEAVES, dtype=jnp.int32)
    column = jnp.broadcast_to(index[None, :, None], (GROUPS, GLEAVES, NEAR_MAX))
    offsets = jax.random.randint(key_off, (GROUPS, GLEAVES, NEAR_MAX), -REACH, REACH + 1, dtype=jnp.int32)
    sources = jnp.clip(column + offsets, 0, GLEAVES - 1)
    row_index = jnp.broadcast_to(index[None, :], (GROUPS, GLEAVES))
    second = jnp.where(row_index + REACH < GLEAVES, row_index + REACH, row_index - REACH)
    sources = sources.at[:, :, 0].set(row_index)
    sources = sources.at[:, :, 1].set(second)
    counts = jax.random.randint(key_count, (GROUPS, GLEAVES), 2, NEAR_MAX + 1, dtype=jnp.int32)
    counts = counts.at[:, 0].set(NEAR_MAX)
    return (sources, counts)


def draw_near_src(key, part):
    return near_lists(key)[0]


def draw_near_count(key, part):
    return near_lists(key)[1]


def distant(key, rows, slots, reach):
    key_sign, key_dist = jax.random.split(key, 2)
    index = jnp.broadcast_to(jnp.arange(rows, dtype=jnp.int32)[None, :, None], (GROUPS, rows, slots))
    signs = jax.random.randint(key_sign, (GROUPS, rows, slots), 0, 2, dtype=jnp.int32) * 2 - 1
    dists = jax.random.randint(key_dist, (GROUPS, rows, slots), 2, reach + 1, dtype=jnp.int32)
    forward = index + signs * dists
    inside = (forward >= 0) & (forward < rows)
    return jnp.where(inside, forward, index - signs * dists)


def draw_far_src(key, part):
    return distant(jax.random.fold_in(key, 23), GLEAVES, FAR, REACH)


def draw_mid_src(key, part):
    return distant(jax.random.fold_in(key, 37), GMIDS, MFAR, MD)


def block_levels(key, extent, pieces, smallest, top_value):
    def one(position, blocks):
        draws = jax.random.uniform(jax.random.fold_in(jax.random.fold_in(key, 6), position), (blocks,), jnp.float32, smallest / len(pieces), top_value / len(pieces))
        return jnp.repeat(jnp.exp(draws), extent[position] // blocks).reshape((-1,) + (1,) * (len(extent) - position - 1))

    factor_of = one(*pieces[0])
    for cut in pieces[1:]:
        factor_of = factor_of * one(*cut)
    return factor_of


def centred(own_key, shape, deviation, bound, shards=(), held_as=jnp.bfloat16):
    values = jax.random.normal(own_key, shape, jnp.float32) * deviation
    if len(shards) > 0:
        values = block_levels(own_key, shape, shards, -0.22, 0.18) * values
    return jnp.clip(values, min=-bound, max=bound).astype(held_as)


def setup_inputs(seed: int = 0) -> dict:
    keys = jax.random.split(jax.random.key(seed), 18)
    charges = centred(keys[0], (GROUPS, GLEAVES, LEAF, RHS), 1.0, 6.0, ((0, 4), (1, 8)))
    leaf_row_basis = centred(keys[1], (GROUPS, GLEAVES, LEAF, RANK), LEAF ** -0.5, 0.75, ((0, 4), (1, 8)))
    leaf_column_basis = centred(keys[2], (GROUPS, GLEAVES, LEAF, RANK), RANK ** -0.5, 0.75, ((0, 4), (1, 8)))
    near_blocks = centred(keys[3], (GROUPS, GLEAVES, NEAR_MAX, LEAF, LEAF), LEAF ** -0.5, 0.75, ((0, 4), (1, 8)))
    near_src = draw_near_src(jax.random.fold_in(keys[17], 71), 0)
    near_count = draw_near_count(jax.random.fold_in(keys[17], 71), 0)
    leaf_coupling = centred(keys[6], (GROUPS, GLEAVES, FAR, RANK, RANK), RANK ** -0.5, 0.75, ((0, 4), (1, 8)))
    far_src = draw_far_src(jax.random.fold_in(keys[17], 71), 0)
    up_leaf = centred(keys[8], (GROUPS, GLEAVES, RANK, RANK), (4 * RANK) ** -0.5, 0.375, ((0, 4), (1, 8)))
    column_transfer_leaf = centred(keys[9], (GROUPS, GLEAVES, RANK, RANK), RANK ** -0.5, 0.75, ((0, 4), (1, 8)))
    mid_coupling = centred(keys[10], (GROUPS, GMIDS, MFAR, RANK, RANK), RANK ** -0.5, 0.75, ((0, 4), (1, 8)))
    mid_src = draw_mid_src(jax.random.fold_in(keys[17], 71), 0)
    up_mid = centred(keys[12], (GROUPS, GMIDS, RANK, RANK), (MD * RANK) ** -0.5, 0.3125, ((0, 4), (1, 8)))
    down_mid = centred(keys[13], (GROUPS, GMIDS, RANK, RANK), RANK ** -0.5, 0.75, ((0, 4), (1, 8)))
    up_top = centred(keys[14], (GROUPS, N_WIDE, RANK, RANK), (N_WIDE * RANK) ** -0.5, 0.25, ((0, 4), (1, 8)))
    down_top = centred(keys[15], (GROUPS, N_WIDE, RANK, RANK), RANK ** -0.5, 0.75, ((0, 4), (1, 8)))
    top_coupling = centred(keys[16], (GROUPS, GROUPS, RANK, RANK), RANK ** -0.5, 0.75, ((0, 4),))
    return dict(charges=charges, leaf_row_basis=leaf_row_basis, leaf_column_basis=leaf_column_basis, near_blocks=near_blocks, near_src=near_src, near_count=near_count, leaf_coupling=leaf_coupling, far_src=far_src, up_leaf=up_leaf, column_transfer_leaf=column_transfer_leaf, mid_coupling=mid_coupling, mid_src=mid_src, up_mid=up_mid, down_mid=down_mid, up_top=up_top, down_top=down_top, top_coupling=top_coupling)


def broaden_rows(array):
    return array.astype(jnp.float32)


def upward(charges, leaf_row_basis, up_leaf, up_mid, up_top):
    leaf_count = charges.shape[0]
    mid_count = leaf_count // 4
    wide_count = up_top.shape[0]
    per_device = mid_count // wide_count
    skeleton_leaf = jnp.einsum("mwl,mwv->mlv", broaden_rows(leaf_row_basis), broaden_rows(charges)).astype(jnp.bfloat16)
    skel_mid = jnp.einsum("mqab,mqac->mbc", broaden_rows(up_leaf).reshape(mid_count, 4, RANK, RANK),
                          broaden_rows(skeleton_leaf).reshape(mid_count, 4, RANK, RHS)).astype(jnp.bfloat16)
    skel_dev = jnp.einsum("wjab,wjac->wbc", broaden_rows(up_mid).reshape(wide_count, per_device, RANK, RANK),
                          broaden_rows(skel_mid).reshape(wide_count, per_device, RANK, RHS)).astype(jnp.bfloat16)
    group_skel = jnp.einsum("wab,wac->bc", broaden_rows(up_top), broaden_rows(skel_dev)).astype(jnp.bfloat16)
    return skeleton_leaf, skel_mid, group_skel


def downward(charges, leaf_column_basis, near_blocks, near_src, near_count, leaf_coupling, far_src, column_transfer_leaf,
             mid_coupling, mid_src, down_mid, down_top, skeleton_leaf, skel_mid, top_part):
    wide_count = down_top.shape[0]
    per_device = skel_mid.shape[0] // wide_count
    down_dev = jnp.einsum("wab,bc->wac", broaden_rows(down_top), broaden_rows(top_part)).astype(jnp.bfloat16)
    middle_downward_pass = (jnp.einsum("jkab,jkac->jbc", broaden_rows(mid_coupling), broaden_rows(skel_mid[mid_src]))
                + jnp.einsum("jab,jbc->jac", broaden_rows(down_mid), broaden_rows(jnp.repeat(down_dev, per_device, axis=0)))
                ).astype(jnp.bfloat16)
    leaf_downward_pass = (jnp.einsum("tkab,tkac->tbc", broaden_rows(leaf_coupling), broaden_rows(skeleton_leaf[far_src]))
                 + jnp.einsum("ruy,ryv->ruv", broaden_rows(column_transfer_leaf), broaden_rows(jnp.repeat(middle_downward_pass, 4, axis=0)))
                 ).astype(jnp.bfloat16)
    live_slot = jnp.arange(NEAR_MAX, dtype=jnp.int32)[None, :] < near_count[:, None]
    gathered = jnp.where(live_slot[:, :, None, None], broaden_rows(charges[near_src]), 0.0)
    near_part = jnp.einsum("tkab,tkac->tbc", broaden_rows(near_blocks), gathered)
    far_field_part = jnp.einsum("eiu,eug->eig", broaden_rows(leaf_column_basis), broaden_rows(leaf_downward_pass))
    return (near_part + far_field_part).astype(jnp.bfloat16)


def reference(charges, leaf_row_basis, leaf_column_basis, near_blocks, near_src, near_count, leaf_coupling, far_src,
              up_leaf, column_transfer_leaf, mid_coupling, mid_src, up_mid, down_mid, up_top, down_top, top_coupling):
    skeleton_leaf, skel_mid, group_skel = lax.map(lambda items: upward(*items),
                                              (charges, leaf_row_basis, up_leaf, up_mid, up_top))
    group_ids = jnp.arange(GROUPS, dtype=jnp.int32)
    other_groups = group_ids[:, None] != group_ids[None, :]
    top_part = jnp.einsum("ghab,hac->gbc", jnp.where(other_groups[:, :, None, None], broaden_rows(top_coupling), 0.0),
                          broaden_rows(group_skel)).astype(jnp.bfloat16)
    return lax.map(lambda items: downward(*items),
                   (charges, leaf_column_basis, near_blocks, near_src, near_count, leaf_coupling, far_src, column_transfer_leaf,
                    mid_coupling, mid_src, down_mid, down_top, skeleton_leaf, skel_mid, top_part))
```

```python
import functools

import jax
import jax.numpy as jnp
from jax import lax
from jax.experimental import pallas as pl
from jax.experimental.pallas import tpu as pltpu
from jax.sharding import PartitionSpec as P

REACH = 8
MREACH = 6
F32 = jnp.float32
BF16 = jnp.bfloat16
NN = (((1,), (0,)), ((), ()))
NT = (((1,), (1,)), ((), ()))


def nn(a, b):
    return lax.dot_general(a, b, NN, preferred_element_type=F32)


def nt(a, b):
    return lax.dot_general(a, b, NT, preferred_element_type=F32)


def pack(a, b):
    return jnp.concatenate([a, b], axis=1)


def up_kernel(c_ref, r_ref, ul_ref, um_ref, ut_ref, ct_ref, st_ref, mt_ref, hl_ref, hr_ref, dt_ref):
    n = c_ref.shape[0]
    mids = um_ref.shape[0]
    w = c_ref.shape[1]
    eye = (
        lax.broadcasted_iota(jnp.int32, (w, w), 0) == lax.broadcasted_iota(jnp.int32, (w, w), 1)
    ).astype(F32).astype(BF16)
    dev = None
    for m in range(mids):
        acc = None
        for q in range(4):
            i = 4 * m + q
            ct = nt(eye, c_ref[i]).astype(BF16)
            ct_ref[i] = ct
            st = nn(ct, r_ref[i]).astype(BF16)
            st_ref[i] = st
            part = nn(st, ul_ref[i])
            acc = part if acc is None else acc + part
        mt = acc.astype(BF16)
        mt_ref[m] = mt
        part = nn(mt, um_ref[m])
        dev = part if dev is None else dev + part
    term = nn(dev.astype(BF16), ut_ref[0])
    h = term.shape[0] // 2
    dt_ref[...] = pack(term[:h], term[h:]).astype(BF16)
    half = REACH // 2
    for k in range(half):
        hl_ref[k] = pack(ct_ref[2 * k], ct_ref[2 * k + 1])
        hl_ref[half + k] = pack(st_ref[2 * k], st_ref[2 * k + 1])
        e = n - REACH + 2 * k
        hr_ref[k] = pack(ct_ref[e], ct_ref[e + 1])
        hr_ref[half + k] = pack(st_ref[e], st_ref[e + 1])
    for k in range(MREACH // 2):
        hl_ref[2 * half + k] = pack(mt_ref[2 * k], mt_ref[2 * k + 1])
        e = mids - MREACH + 2 * k
        hr_ref[2 * half + k] = pack(mt_ref[e], mt_ref[e + 1])


def unpack(ref, k, tab, at):
    both = ref[k]
    h = both.shape[1] // 2
    tab[at] = both[:, :h]
    tab[at + 1] = both[:, h:]


def far_kernel(
    ni_ref, fi_ref, mi_ref, ct_ref, st_ref, mt_ref, fl_ref, fr_ref, nb_ref, lc_ref, mc_ref,
    near_ref, lp_ref, mp_ref, ctab, stab, mtab,
):
    n = ct_ref.shape[0]
    mids = mt_ref.shape[0]
    half = REACH // 2
    for i in range(n):
        ctab[REACH + i] = ct_ref[i]
        stab[REACH + i] = st_ref[i]
    for i in range(mids):
        mtab[MREACH + i] = mt_ref[i]
    ctab[n + 2 * REACH] = jnp.zeros(ctab.shape[1:], BF16)
    for k in range(half):
        unpack(fl_ref, k, ctab, 2 * k)
        unpack(fl_ref, half + k, stab, 2 * k)
        unpack(fr_ref, k, ctab, n + REACH + 2 * k)
        unpack(fr_ref, half + k, stab, n + REACH + 2 * k)
    for k in range(MREACH // 2):
        unpack(fl_ref, 2 * half + k, mtab, 2 * k)
        unpack(fr_ref, 2 * half + k, mtab, mids + MREACH + 2 * k)

    @pl.loop(0, n)
    def _(i):
        acc = None
        for k in range(nb_ref.shape[1]):
            part = nn(ctab[ni_ref[i, k]], nb_ref[i, k])
            acc = part if acc is None else acc + part
        near_ref[i] = jnp.transpose(acc)
        acc = None
        for k in range(lc_ref.shape[1]):
            part = nn(stab[fi_ref[i, k]], lc_ref[i, k])
            acc = part if acc is None else acc + part
        lp_ref[i] = acc

    for j in range(mids):
        acc = None
        for k in range(mc_ref.shape[1]):
            part = nn(mtab[mi_ref[j, k]], mc_ref[j, k])
            acc = part if acc is None else acc + part
        mp_ref[j] = acc


def down_kernel(hs_ref, g_ref, tc_ref, dtop_ref, dm_ref, tl_ref, cb_ref, near_ref, lp_ref, mp_ref, out_ref):
    mids = dm_ref.shape[0]
    acc = None
    for k in range(g_ref.shape[0]):
        g = g_ref[k]
        h = g.shape[1] // 2
        gt = jnp.concatenate([g[:, :h], g[:, h:]], axis=0)
        part = nn(gt, tc_ref[hs_ref[k]])
        acc = part if acc is None else acc + part
    dd = nt(acc.astype(BF16), dtop_ref[0]).astype(BF16)
    for m in range(mids):
        md = (mp_ref[m] + nt(dd, dm_ref[m])).astype(BF16)
        for q in range(4):
            i = 4 * m + q
            ld = (lp_ref[i] + nt(md, tl_ref[i])).astype(BF16)
            out_ref[i] = (near_ref[i] + nt(cb_ref[i], ld)).astype(BF16)


def swap(pairs_of, count):
    return [(i, pairs_of(i)) for i in range(count)]


def on_device(
    charges, leaf_row_basis, leaf_column_basis, near_blocks, near_src, near_count, leaf_coupling, far_src,
    up_leaf, column_transfer_leaf, mid_coupling, mid_src, up_mid, down_mid, up_top, down_top, top_coupling,
):
    n, w, v = charges.shape[1:]
    r = leaf_row_basis.shape[3]
    mids = up_mid.shape[1]
    wide, narrow = lax.axis_size("wide"), lax.axis_size("narrow")
    both = ("wide", "narrow")
    total = wide * narrow
    pos = lax.axis_index("wide")
    me = lax.axis_index("narrow")
    pairs = REACH + MREACH // 2

    def shp(*s, t=BF16):
        return jax.ShapeDtypeStruct(s, t)

    ct, st, mt, hl, hr, term = pl.pallas_call(
        up_kernel,
        out_shape=[shp(n, v, w), shp(n, v, r), shp(mids, v, r), shp(pairs, v, 2 * r), shp(pairs, v, 2 * r), shp(v // 2, 2 * r)],
        compiler_params=pltpu.CompilerParams(vmem_limit_bytes=16 << 20),
        name="up",
    )(charges[0], leaf_row_basis[0], up_leaf[0], up_mid[0], up_top[0])

    from_left = lax.ppermute(hr, "wide", [(i, i + 1) for i in range(wide - 1)])
    from_right = lax.ppermute(hl, "wide", [(i + 1, i) for i in range(wide - 1)])

    def xor(x, dw, dn):
        return lax.ppermute(x, both, [(i * narrow + j, (i ^ dw) * narrow + (j ^ dn)) for i in range(wide) for j in range(narrow)])

    f = term.astype(F32)
    own = f + xor(term, 1, 0).astype(F32)
    other = xor(term, 0, 2).astype(F32) + xor(term, 1, 2).astype(F32)
    have = jnp.stack([own, other]).astype(BF16)
    bit = 2
    while bit < wide:
        got = have.astype(F32) + xor(have, bit, 0).astype(F32)
        if 2 * bit < wide:
            got = got + xor(have, 2 * bit, 0).astype(F32) + xor(have, 3 * bit, 0).astype(F32)
        have = got.astype(BF16)
        bit *= 4
    over = xor(have, 0, 1)
    groups = jnp.concatenate([have[1:], over], axis=0)
    hs = jnp.stack([me ^ 2, me ^ 1, me ^ 3]).astype(jnp.int32)

    live = jnp.arange(near_src.shape[2], dtype=jnp.int32)[None, :] < near_count[0][:, None]
    ni = jnp.where(live, near_src[0] - (pos * n - REACH), n + 2 * REACH)
    fi = far_src[0] - (pos * n - REACH)
    mi = mid_src[0] - (pos * mids - MREACH)

    smem = pl.BlockSpec(memory_space=pltpu.SMEM)
    vm = pl.BlockSpec(memory_space=pltpu.VMEM)
    near, lp, mp = pl.pallas_call(
        far_kernel,
        in_specs=[smem] * 3 + [vm] * 8,
        out_shape=[shp(n, w, v, t=F32), shp(n, v, r, t=F32), shp(mids, v, r, t=F32)],
        scratch_shapes=[
            pltpu.VMEM((n + 2 * REACH + 1, v, w), BF16),
            pltpu.VMEM((n + 2 * REACH, v, r), BF16),
            pltpu.VMEM((mids + 2 * MREACH, v, r), BF16),
        ],
        compiler_params=pltpu.CompilerParams(vmem_limit_bytes=32 << 20),
        name="far",
    )(ni, fi, mi, ct, st, mt, from_left, from_right, near_blocks[0], leaf_coupling[0], mid_coupling[0])

    out = pl.pallas_call(
        down_kernel,
        in_specs=[smem] + [vm] * 9,
        out_shape=shp(n, w, v),
        compiler_params=pltpu.CompilerParams(vmem_limit_bytes=16 << 20),
        name="down",
    )(hs, groups, top_coupling[0], down_top[0], down_mid[0], column_transfer_leaf[0], leaf_column_basis[0], near, lp, mp)
    return out[None]


def solution(mesh):
    leaf = P("narrow", "wide", None, None)
    block = P("narrow", "wide", None, None, None)
    lists = P("narrow", "wide", None)
    return jax.shard_map(
        on_device,
        mesh=mesh,
        in_specs=(
            leaf, leaf, leaf, block, lists, P("narrow", "wide"), block, lists,
            leaf, leaf, block, lists, leaf, leaf, leaf, leaf, P("narrow", None, None, None),
        ),
        out_specs=leaf,
        check_vma=False,
    )
```

```python
import functools

import jax
import jax.numpy as jnp
from jax import lax
from jax.experimental import pallas as pl
from jax.experimental.pallas import tpu as pltpu
from jax.sharding import PartitionSpec as P

REACH = 8
MREACH = 6
F32 = jnp.float32
BF16 = jnp.bfloat16
NN = (((1,), (0,)), ((), ()))
NT = (((1,), (1,)), ((), ()))


def nn(a, b):
    return lax.dot_general(a, b, NN, preferred_element_type=F32)


def nt(a, b):
    return lax.dot_general(a, b, NT, preferred_element_type=F32)


def beside(*parts):
    return jnp.concatenate(parts, axis=1)


def rows(ref, *at):
    x = ref[at]
    return x.reshape(-1, x.shape[-1])


def in_hbm(x):
    return pltpu.with_memory_space_constraint(x, pltpu.HBM)


def up_kernel(c_hbm, r_hbm, ul_hbm, um_hbm, ut_hbm, cp_ref, sp_ref, mp_ref, e0_ref, e1_ref, dt_ref,
              c_ref, r_ref, ul_ref, um_ref, ut_ref, sems):
    n, w = c_ref.shape[:2]
    mids = um_ref.shape[0]
    cut = n // 2
    copies = []
    for h in range(2):
        part = pl.ds(h * cut, cut)
        copies.append([
            pltpu.make_async_copy(src.at[part], dst.at[part], sems.at[3 * h + j])
            for j, (src, dst) in enumerate(((c_hbm, c_ref), (r_hbm, r_ref), (ul_hbm, ul_ref)))
        ])
    tail = [pltpu.make_async_copy(um_hbm, um_ref, sems.at[6]), pltpu.make_async_copy(ut_hbm, ut_ref, sems.at[7])]
    for group in copies + [tail]:
        for copy in group:
            copy.start()
    eye = (
        lax.broadcasted_iota(jnp.int32, (w, w), 0) == lax.broadcasted_iota(jnp.int32, (w, w), 1)
    ).astype(F32).astype(BF16)
    zero = jnp.zeros((w, w), BF16)
    zeros = jnp.zeros((w, 2 * w), BF16)
    mid = []
    for m in range(mids):
        for h in range(2):
            if 4 * m == h * cut:
                for copy in copies[h]:
                    copy.wait()
        i = 4 * m
        ct = nt(eye, rows(c_ref, pl.ds(i, 4))).astype(BF16)
        cp_ref[2 * m] = ct[:, : 2 * w]
        cp_ref[2 * m + 1] = ct[:, 2 * w :]
        blocks = jnp.concatenate([
            beside(beside(r_ref[i], zero), zeros),
            beside(beside(zero, r_ref[i + 1]), zeros),
            beside(zeros, beside(r_ref[i + 2], zero)),
            beside(zeros, beside(zero, r_ref[i + 3])),
        ], axis=0)
        st = nn(ct, blocks).astype(BF16)
        sp_ref[2 * m] = st[:, : 2 * w]
        sp_ref[2 * m + 1] = st[:, 2 * w :]
        mid.append(nn(st, rows(ul_ref, pl.ds(i, 4))))
    for m in range(mids // 2):
        mp_ref[m] = beside(mid[2 * m], mid[2 * m + 1]).astype(BF16)
    for copy in tail:
        copy.wait()
    dev = nn(beside(*[mp_ref[m] for m in range(mids // 2)]), rows(um_ref, pl.ds(0, mids)))
    term = nn(dev.astype(BF16), ut_ref[0])
    h = term.shape[0] // 2
    dt_ref[...] = beside(term[:h], term[h:]).astype(BF16)
    odd = lax.axis_index("wide") % 2
    half, mhalf = REACH // 2, MREACH // 2
    for e_ref, right in ((e0_ref, 1 - odd), (e1_ref, odd)):
        at = right * (n // 2 - half)
        mat = right * (mids // 2 - mhalf)
        for k in range(half):
            e_ref[k] = cp_ref[at + k]
            e_ref[half + k] = sp_ref[at + k]
        for k in range(mhalf):
            e_ref[2 * half + k] = mp_ref[mat + k]


def far_kernel(near_hbm, count_hbm, far_hbm, mid_hbm, cp_ref, sp_ref, mp_ref, f0_ref, f1_ref, nb_hbm, lc_hbm, mc_hbm,
               near_ref, lf_ref, mf_ref, ctab, stab, mtab, ni_ref, nc_ref, fi_ref, mi_ref, nb_ref, lc_ref, mc_ref,
               small, big):
    n = nb_ref.shape[0]
    slots, fars, mfars = nb_ref.shape[1], lc_ref.shape[1], mc_ref.shape[1]
    mids = mc_ref.shape[0]
    lists = [
        pltpu.make_async_copy(src, dst, small.at[j])
        for j, (src, dst) in enumerate(((near_hbm, ni_ref), (count_hbm, nc_ref), (far_hbm, fi_ref), (mid_hbm, mi_ref)))
    ]
    for copy in lists:
        copy.start()
    whole = pltpu.make_async_copy(mc_hbm, mc_ref, small.at[4])
    whole.start()
    groups = big.shape[1]
    step = n // groups

    def chunk(g):
        part = pl.ds(g * step, step)
        return (
            pltpu.make_async_copy(nb_hbm.at[part], nb_ref.at[part], big.at[0, g]),
            pltpu.make_async_copy(lc_hbm.at[part], lc_ref.at[part], big.at[1, g]),
        )

    for g in range(groups):
        for copy in chunk(g):
            copy.start()
    w = ctab.shape[1]
    lo = lax.broadcasted_iota(jnp.int32, (w, 2 * w), 1) < w
    odd = lax.axis_index("wide") % 2
    pos = lax.axis_index("wide")

    def double(pair, tab, at):
        turned = jnp.concatenate([pair[:, w:], pair[:, :w]], axis=1)
        tab[at] = jnp.where(lo, pair, turned)
        tab[at + 1] = jnp.where(lo, turned, pair)

    half, mhalf = REACH // 2, MREACH // 2

    @pl.loop(0, n // 2)
    def _(k):
        double(cp_ref[k], ctab, REACH + 2 * k)
        double(sp_ref[k], stab, REACH + 2 * k)

    for k in range(mids // 2):
        double(mp_ref[k], mtab, MREACH + 2 * k)
    ctab[n + 2 * REACH] = jnp.zeros(ctab.shape[1:], BF16)
    for f_ref, right in ((f0_ref, 1 - odd), (f1_ref, odd)):
        at = right * (n + REACH)
        mat = right * (mids + MREACH)

        @pl.loop(0, half)
        def _(k):
            double(f_ref[k], ctab, at + 2 * k)
            double(f_ref[half + k], stab, at + 2 * k)

        for k in range(mhalf):
            double(f_ref[2 * half + k], mtab, mat + 2 * k)
    for copy in lists:
        copy.wait()
    base, mbase = pos * n - REACH, pos * mids - MREACH

    def side(tab, idx):
        return beside(*[jnp.where(lo, tab[idx[k]], tab[idx[k + 1]]) for k in range(0, len(idx), 2)])

    whole.wait()
    for j in range(mids):
        idx = [mi_ref[j, 0, k] - mbase for k in range(mfars)]
        mf_ref[j] = jnp.transpose(nn(side(mtab, idx), rows(mc_ref, j)))

    @pl.loop(0, groups)
    def _(g):
        for copy in chunk(g):
            copy.wait()
        for q in range(step):
            i = g * step + q
            live = nc_ref[0, i]
            idx = [jnp.where(k < live, ni_ref[k, i] - base, n + 2 * REACH) for k in range(slots)]
            near_ref[i] = jnp.transpose(nn(side(ctab, idx), rows(nb_ref, i)))
            idx = [fi_ref[k, 0, i] - base for k in range(fars)]
            lf_ref[i] = jnp.transpose(nn(side(stab, idx), rows(lc_ref, i)))


def down_kernel(own_ref, over_ref, tc_ref, dtop_ref, dm_ref, tl_ref, cb_ref, near_ref, lf_ref, mf_ref, out_ref):
    mids = dm_ref.shape[0]
    me = lax.axis_index("narrow")
    acc = None
    for ref, k, h in ((own_ref, 1, me ^ 2), (over_ref, 0, me ^ 1), (over_ref, 1, me ^ 3)):
        g = ref[k]
        c = g.shape[1] // 2
        gt = jnp.concatenate([g[:, :c], g[:, c:]], axis=0)
        part = nn(gt, tc_ref[h])
        acc = part if acc is None else acc + part
    dd = nt(dtop_ref[0], acc.astype(BF16)).astype(BF16)
    down = nn(rows(dm_ref, pl.ds(0, mids)), dd)
    r = dd.shape[0]
    for m in range(mids):
        md = (mf_ref[m] + down[m * r : (m + 1) * r]).astype(BF16)
        ld = nn(rows(tl_ref, pl.ds(4 * m, 4)), md)
        for q in range(4):
            i = 4 * m + q
            lq = (lf_ref[i] + ld[q * r : (q + 1) * r]).astype(BF16)
            out_ref[i] = (near_ref[i] + nn(cb_ref[i], lq)).astype(BF16)


def on_device(
    charges, leaf_row_basis, leaf_column_basis, near_blocks, near_src, near_count, leaf_coupling, far_src,
    up_leaf, column_transfer_leaf, mid_coupling, mid_src, up_mid, down_mid, up_top, down_top, top_coupling,
):
    n, w, v = charges.shape[1:]
    mids = up_mid.shape[1]
    wide, narrow = lax.axis_size("wide"), lax.axis_size("narrow")
    both = ("wide", "narrow")
    pairs = REACH + MREACH // 2
    slots, fars, mfars = near_src.shape[2], far_src.shape[2], mid_src.shape[2]
    hbm = pl.BlockSpec(memory_space=pltpu.HBM)
    vm = pl.BlockSpec(memory_space=pltpu.VMEM)
    dma = pltpu.SemaphoreType.DMA

    def shp(*s, t=BF16):
        return jax.ShapeDtypeStruct(s, t)

    cp, sp, mp, e0, e1, term = pl.pallas_call(
        up_kernel,
        in_specs=[hbm] * 5,
        out_specs=[vm] * 6,
        out_shape=[shp(n // 2, v, 2 * w), shp(n // 2, v, 2 * w), shp(mids // 2, v, 2 * w),
                   shp(pairs, v, 2 * w), shp(pairs, v, 2 * w), shp(v // 2, 2 * w)],
        scratch_shapes=[
            pltpu.VMEM((n, w, v), BF16), pltpu.VMEM((n, w, v), BF16), pltpu.VMEM((n, w, v), BF16),
            pltpu.VMEM((mids, w, v), BF16), pltpu.VMEM((1, w, v), BF16), dma((8,)),
        ],
        compiler_params=pltpu.CompilerParams(vmem_limit_bytes=16 << 20),
        cost_estimate=pl.CostEstimate(flops=30_000_000, bytes_accessed=4_000_000, transcendentals=0),
        name="up",
    )(*map(in_hbm, (charges[0], leaf_row_basis[0], up_leaf[0], up_mid[0], up_top[0])))

    def xor(x, dw, dn):
        return lax.ppermute(x, both, [(i * narrow + j, (i ^ dw) * narrow + (j ^ dn)) for i in range(wide) for j in range(narrow)])

    f = term.astype(F32)
    own = f + xor(term, 1, 0).astype(F32)
    other = xor(term, 0, 2).astype(F32) + xor(term, 1, 2).astype(F32)
    f0 = lax.ppermute(e0, "wide", [(i, i ^ 1) for i in range(wide)])
    f1 = lax.ppermute(e1, "wide", [(i, ((i + 1) ^ 1) - 1) for i in range(1, wide - 1)])
    have = jnp.stack([own, other]).astype(BF16)
    bit = 2
    while bit < wide:
        got = have.astype(F32) + xor(have, bit, 0).astype(F32)
        if 2 * bit < wide:
            got = got + xor(have, 2 * bit, 0).astype(F32) + xor(have, 3 * bit, 0).astype(F32)
        have = got.astype(BF16)
        bit *= 4
    over = xor(have, 0, 1)

    near_list = jnp.transpose(near_src, (0, 2, 1))[0]
    far_list = jnp.transpose(far_src, (2, 0, 1))
    mid_list = jnp.transpose(mid_src, (1, 0, 2))
    near, lf, mf = pl.pallas_call(
        far_kernel,
        in_specs=[hbm] * 4 + [vm] * 5 + [hbm] * 3,
        out_specs=[vm] * 3,
        out_shape=[shp(n, w, v, t=F32), shp(n, w, v, t=F32), shp(mids, w, v, t=F32)],
        scratch_shapes=[
            pltpu.VMEM((n + 2 * REACH + 1, v, 2 * w), BF16),
            pltpu.VMEM((n + 2 * REACH, v, 2 * w), BF16),
            pltpu.VMEM((mids + 2 * MREACH, v, 2 * w), BF16),
            pltpu.SMEM((slots, n), jnp.int32), pltpu.SMEM((1, n), jnp.int32),
            pltpu.SMEM((fars, 1, n), jnp.int32), pltpu.SMEM((mids, 1, mfars), jnp.int32),
            pltpu.VMEM((n, slots, w, v), BF16), pltpu.VMEM((n, fars, w, v), BF16), pltpu.VMEM((mids, mfars, w, v), BF16),
            dma((5,)), dma((2, mids)),
        ],
        compiler_params=pltpu.CompilerParams(vmem_limit_bytes=24 << 20),
        cost_estimate=pl.CostEstimate(flops=200_000_000, bytes_accessed=12_000_000, transcendentals=0),
        name="far",
    )(*map(in_hbm, (near_list, near_count, far_list, mid_list)), cp, sp, mp, f0, f1,
      *map(in_hbm, (near_blocks[0], leaf_coupling[0], mid_coupling[0])))

    out = pl.pallas_call(
        down_kernel,
        in_specs=[vm] * 10,
        out_shape=shp(n, w, v),
        compiler_params=pltpu.CompilerParams(vmem_limit_bytes=16 << 20),
        cost_estimate=pl.CostEstimate(flops=30_000_000, bytes_accessed=4_000_000, transcendentals=0),
        name="down",
    )(have, over, top_coupling[0], down_top[0], down_mid[0], column_transfer_leaf[0], leaf_column_basis[0], near, lf, mf)
    return out[None]


def solution(mesh):
    leaf = P("narrow", "wide", None, None)
    block = P("narrow", "wide", None, None, None)
    lists = P("narrow", "wide", None)
    return jax.shard_map(
        on_device,
        mesh=mesh,
        in_specs=(
            leaf, leaf, leaf, block, lists, P("narrow", "wide"), block, lists,
            leaf, leaf, block, lists, leaf, leaf, leaf, leaf, P("narrow", None, None, None),
        ),
        out_specs=leaf,
        check_vma=False,
    )
```

```python
import jax
import jax.numpy as jnp
from jax import lax
from jax.experimental import pallas as pl
from jax.experimental.pallas import tpu as pltpu
from jax.sharding import PartitionSpec as P


REACH = 8
MREACH = 6
F32 = jnp.float32
BF16 = jnp.bfloat16
NN = (((1,), (0,)), ((), ()))
NT = (((1,), (1,)), ((), ()))


def nn(a, b):
    return lax.dot_general(a, b, NN, preferred_element_type=F32)


def nt(a, b):
    return lax.dot_general(a, b, NT, preferred_element_type=F32)


def beside(*parts):
    return jnp.concatenate(parts, axis=1)


def rows(ref, *at):
    x = ref[at]
    return x.reshape(-1, x.shape[-1])


def in_hbm(x):
    return pltpu.with_memory_space_constraint(x, pltpu.HBM)


def up_kernel(c_hbm, r_hbm, ul_hbm, um_hbm, ut_hbm, nb_hbm, lc_hbm, mc_hbm,
              cp_ref, sp_ref, mp_ref, e0_ref, e1_ref, dt_ref, nbi_ref, lci_ref, lcl_ref, mc_ref,
              c_ref, r_ref, ul_ref, um_ref, ut_ref, sems):
    n, w = c_ref.shape[:2]
    mids = um_ref.shape[0]
    copies = [
        pltpu.make_async_copy(src, dst, sems.at[j])
        for j, (src, dst) in enumerate(
            ((ut_hbm, ut_ref), (um_hbm, um_ref), (c_hbm, c_ref), (r_hbm, r_ref), (ul_hbm, ul_ref)))
    ]
    inside = pl.ds(REACH, nbi_ref.shape[0])
    later = [
        pltpu.make_async_copy(nb_hbm.at[inside], nbi_ref, sems.at[5]),
        pltpu.make_async_copy(lc_hbm.at[inside], lci_ref, sems.at[6]),
        pltpu.make_async_copy(mc_hbm, mc_ref, sems.at[7]),
        pltpu.make_async_copy(lc_hbm.at[pl.ds(0, REACH)], lcl_ref, sems.at[8]),
    ]
    for copy in copies + later:
        copy.start()
    eye = (
        lax.broadcasted_iota(jnp.int32, (w, w), 0) == lax.broadcasted_iota(jnp.int32, (w, w), 1)
    ).astype(F32).astype(BF16)
    zero = jnp.zeros((w, w), BF16)
    zeros = jnp.zeros((w, 2 * w), BF16)
    odd = lax.axis_index("wide") % 2
    for copy in copies:
        copy.wait()
    top = nn(rows(um_ref, pl.ds(0, mids)), ut_ref[0]).astype(BF16)
    cts = [nt(eye, rows(c_ref, pl.ds(4 * m, 4))).astype(BF16) for m in range(mids)]
    sts = []
    for m in range(mids):
        i = 4 * m
        blocks = jnp.concatenate([
            beside(beside(r_ref[i], zero), zeros),
            beside(beside(zero, r_ref[i + 1]), zeros),
            beside(zeros, beside(r_ref[i + 2], zero)),
            beside(zeros, beside(zero, r_ref[i + 3])),
        ], axis=0)
        sts.append(nn(cts[m], blocks).astype(BF16))
    for m in range(mids):
        cp_ref[2 * m] = cts[m][:, : 2 * w]
        cp_ref[2 * m + 1] = cts[m][:, 2 * w :]
        sp_ref[2 * m] = sts[m][:, : 2 * w]
        sp_ref[2 * m + 1] = sts[m][:, 2 * w :]
    mid = [nn(sts[m], rows(ul_ref, pl.ds(4 * m, 4))) for m in range(mids)]
    pairs = [beside(mid[2 * m], mid[2 * m + 1]).astype(BF16) for m in range(mids // 2)]
    for m in range(mids // 2):
        mp_ref[m] = pairs[m]
    term = nn(beside(*pairs), top)
    h = term.shape[0] // 2
    dt_ref[...] = beside(term[:h], term[h:]).astype(BF16)
    half, mhalf = REACH // 2, MREACH // 2
    for e_ref, right in ((e0_ref, 1 - odd), (e1_ref, odd)):
        at = right * (n // 2 - half)
        mat = right * (mids // 2 - mhalf)
        for k in range(half):
            e_ref[k] = cp_ref[at + k]
            e_ref[half + k] = sp_ref[at + k]
        for k in range(mhalf):
            e_ref[2 * half + k] = mp_ref[mat + k]
    for copy in later:
        copy.wait()


def double(pair, lo, tab, at):
    w = pair.shape[1] // 2
    turned = beside(pair[:, w:], pair[:, :w])
    tab[at] = jnp.where(lo, pair, turned)
    tab[at + 1] = jnp.where(lo, turned, pair)


def low(w):
    return lax.broadcasted_iota(jnp.int32, (w, 2 * w), 1) < w


def side(lo, tab, idx):
    return beside(*[jnp.where(lo, tab[idx[k]], tab[idx[k + 1]]) for k in range(0, len(idx), 2)])


def lists_in(near_hbm, count_hbm, far_hbm, ni_ref, nc_ref, fi_ref, sems):
    return [
        pltpu.make_async_copy(src, dst, sems.at[j])
        for j, (src, dst) in enumerate(((near_hbm, ni_ref), (count_hbm, nc_ref), (far_hbm, fi_ref)))
    ]


def inner_kernel(near_hbm, count_hbm, far_hbm, cp_ref, sp_ref, nb_ref, lc_ref, nb_hbm, lc_hbm,
                 near_ref, lf_ref, c2_ref, s2_ref, nbo_ref, lcr_ref, ni_ref, nc_ref, fi_ref, small, big):
    slots, fars = nb_ref.shape[1], lc_ref.shape[1]
    n = s2_ref.shape[0]
    inside = near_ref.shape[0]
    right = pl.ds(n - REACH, REACH)
    later = [
        pltpu.make_async_copy(nb_hbm.at[pl.ds(0, REACH)], nbo_ref.at[pl.ds(0, REACH)], big.at[0]),
        pltpu.make_async_copy(nb_hbm.at[right], nbo_ref.at[pl.ds(REACH, REACH)], big.at[1]),
        pltpu.make_async_copy(lc_hbm.at[right], lcr_ref, big.at[2]),
    ]
    w = c2_ref.shape[1]
    lists = lists_in(near_hbm, count_hbm, far_hbm, ni_ref, nc_ref, fi_ref, small)
    for copy in lists + later:
        copy.start()
    lo = low(w)

    @pl.loop(0, n // 8)
    def _(g):
        for q in range(4):
            k = 4 * g + q
            double(cp_ref[k], lo, c2_ref, 2 * k)
            double(sp_ref[k], lo, s2_ref, 2 * k)

    c2_ref[n] = jnp.zeros(c2_ref.shape[1:], BF16)
    base = lax.axis_index("wide") * n
    for copy in lists:
        copy.wait()

    @pl.loop(0, inside // 4)
    def _(g):
        for r in range(4):
            q = 4 * g + r
            i = REACH + q
            live = nc_ref[0, i]
            idx = [jnp.where(k < live, ni_ref[k, i] - base, n) for k in range(slots)]
            near_ref[q] = jnp.transpose(nn(side(lo, c2_ref, idx), rows(nb_ref, q)))
            idx = [fi_ref[k, 0, i] - base for k in range(fars)]
            lf_ref[q] = jnp.transpose(nn(side(lo, s2_ref, idx), rows(lc_ref, q)))

    for copy in later:
        copy.wait()


def outer_kernel(near_hbm, count_hbm, far_hbm, c2_ref, s2_ref, f0_ref, f1_ref, nb_ref, lcl_ref, lcr_ref,
                 near_ref, lf_ref, lc_ref, ctab, stab, ni_ref, nc_ref, fi_ref, small, big):
    slots, fars = nb_ref.shape[1], lcl_ref.shape[1]
    n = c2_ref.shape[0] - 1
    w = c2_ref.shape[1]
    copies = lists_in(near_hbm, count_hbm, far_hbm, ni_ref, nc_ref, fi_ref, small) + [
        pltpu.make_async_copy(c2_ref.at[pl.ds(0, n)], ctab.at[pl.ds(REACH, n)], big.at[0]),
        pltpu.make_async_copy(s2_ref, stab.at[pl.ds(REACH, n)], big.at[1]),
        pltpu.make_async_copy(lcl_ref, lc_ref.at[pl.ds(0, REACH)], big.at[2]),
        pltpu.make_async_copy(lcr_ref, lc_ref.at[pl.ds(REACH, REACH)], big.at[3]),
    ]
    for copy in copies:
        copy.start()
    lo = low(w)
    pos = lax.axis_index("wide")
    odd = pos % 2
    half = REACH // 2
    for f_ref, right in ((f0_ref, 1 - odd), (f1_ref, odd)):
        at = right * (n + REACH)
        for k in range(half):
            double(f_ref[k], lo, ctab, at + 2 * k)
            double(f_ref[half + k], lo, stab, at + 2 * k)
    ctab[n + 2 * REACH] = jnp.zeros(ctab.shape[1:], BF16)
    base = pos * n - REACH
    for copy in copies:
        copy.wait()

    @pl.loop(0, 2)
    def _(g):
        for q in range(REACH):
            j = g * REACH + q
            i = g * (n - REACH) + q
            live = nc_ref[0, i]
            idx = [jnp.where(k < live, ni_ref[k, i] - base, n + 2 * REACH) for k in range(slots)]
            near_ref[j] = jnp.transpose(nn(side(lo, ctab, idx), rows(nb_ref, j)))
            idx = [fi_ref[k, 0, i] - base for k in range(fars)]
            lf_ref[j] = jnp.transpose(nn(side(lo, stab, idx), rows(lc_ref, j)))


def middle_kernel(mid_hbm, mp_ref, f0_ref, f1_ref, mc_ref, mf_ref, mtab, mi_ref, small):
    mids, mfars = mc_ref.shape[:2]
    w = mtab.shape[1]
    copy = pltpu.make_async_copy(mid_hbm, mi_ref, small.at[0])
    copy.start()
    lo = low(w)
    pos = lax.axis_index("wide")
    odd = pos % 2
    for k in range(mids // 2):
        double(mp_ref[k], lo, mtab, MREACH + 2 * k)
    for f_ref, right in ((f0_ref, 1 - odd), (f1_ref, odd)):
        for k in range(MREACH // 2):
            double(f_ref[REACH + k], lo, mtab, right * (mids + MREACH) + 2 * k)
    base = pos * mids - MREACH
    copy.wait()
    for j in range(mids):
        idx = [mi_ref[j, 0, k] - base for k in range(mfars)]
        mf_ref[j] = jnp.transpose(nn(side(lo, mtab, idx), rows(mc_ref, j)))


def down_kernel(own_ref, over_ref, tc_ref, dtop_ref, dm_ref, tl_ref, cb_ref, neari_ref, lfi_ref, nearo_ref, lfo_ref, mf_ref,
                out_hbm, out_ref, sems):
    mids = dm_ref.shape[0]
    n = tl_ref.shape[0]
    me = lax.axis_index("narrow")
    acc = None
    for ref, k, h in ((own_ref, 1, me ^ 2), (over_ref, 0, me ^ 1), (over_ref, 1, me ^ 3)):
        g = ref[k]
        c = g.shape[1] // 2
        gt = jnp.concatenate([g[:, :c], g[:, c:]], axis=0)
        part = nn(gt, tc_ref[h])
        acc = part if acc is None else acc + part
    dd = nt(dtop_ref[0], acc.astype(BF16)).astype(BF16)
    down = nn(rows(dm_ref, pl.ds(0, mids)), dd)
    r = dd.shape[0]
    copies = []
    for m in range(mids):
        md = (mf_ref[m] + down[m * r : (m + 1) * r]).astype(BF16)
        ld = nn(rows(tl_ref, pl.ds(4 * m, 4)), md)
        for q in range(4):
            i = 4 * m + q
            if REACH <= i < n - REACH:
                near, lf = neari_ref[i - REACH], lfi_ref[i - REACH]
            else:
                j = i if i < REACH else i - (n - 2 * REACH)
                near, lf = nearo_ref[j], lfo_ref[j]
            lq = (lf + ld[q * r : (q + 1) * r]).astype(BF16)
            out_ref[i] = (near + nn(cb_ref[i], lq)).astype(BF16)
        if m % 2 == 1:
            part = pl.ds(4 * (m - 1), 8)
            copy = pltpu.make_async_copy(out_ref.at[part], out_hbm.at[part], sems.at[m // 2])
            copy.start()
            copies.append(copy)
    for copy in copies:
        copy.wait()


def apply(
    charges, leaf_row_basis, leaf_column_basis, near_blocks, near_src, near_count, leaf_coupling, far_src,
    up_leaf, column_transfer_leaf, mid_coupling, mid_src, up_mid, down_mid, up_top, down_top, top_coupling,
):
    n, w, v = charges.shape[1:]
    mids = up_mid.shape[1]
    wide, narrow = lax.axis_size("wide"), lax.axis_size("narrow")
    both = ("wide", "narrow")
    pairs = REACH + MREACH // 2
    slots, fars, mfars = near_src.shape[2], far_src.shape[2], mid_src.shape[2]
    hbm = pl.BlockSpec(memory_space=pltpu.HBM)
    vm = pl.BlockSpec(memory_space=pltpu.VMEM)
    dma = pltpu.SemaphoreType.DMA

    def shp(*s, t=BF16):
        return jax.ShapeDtypeStruct(s, t)

    inside = n - 2 * REACH
    cp, sp, mp, e0, e1, term, nbi, lci, lcl, mc = pl.pallas_call(
        up_kernel,
        in_specs=[hbm] * 8,
        out_specs=[vm] * 10,
        out_shape=[shp(n // 2, v, 2 * w), shp(n // 2, v, 2 * w), shp(mids // 2, v, 2 * w),
                   shp(pairs, v, 2 * w), shp(pairs, v, 2 * w), shp(v // 2, 2 * w),
                   shp(inside, slots, w, v), shp(inside, fars, w, v), shp(REACH, fars, w, v), shp(mids, mfars, w, v)],
        scratch_shapes=[
            pltpu.VMEM((n, w, v), BF16), pltpu.VMEM((n, w, v), BF16), pltpu.VMEM((n, w, v), BF16),
            pltpu.VMEM((mids, w, v), BF16), pltpu.VMEM((1, w, v), BF16), dma((9,)),
        ],
        compiler_params=pltpu.CompilerParams(vmem_limit_bytes=16 << 20),
        cost_estimate=pl.CostEstimate(flops=30_000_000, bytes_accessed=4_000_000, transcendentals=0),
        name="up",
    )(*map(in_hbm, (charges[0], leaf_row_basis[0], up_leaf[0], up_mid[0], up_top[0],
                  near_blocks[0], leaf_coupling[0], mid_coupling[0])))

    def xor(x, dw, dn):
        return lax.ppermute(x, both, [(i * narrow + j, (i ^ dw) * narrow + (j ^ dn)) for i in range(wide) for j in range(narrow)])

    f0 = lax.ppermute(e0, "wide", [(i, i ^ 1) for i in range(wide)])
    f1 = lax.ppermute(e1, "wide", [(i, (((i + 1) ^ 1) - 1) % wide) for i in range(wide)])
    f = term.astype(F32)
    own = (f + xor(term, 1, 0).astype(F32)).astype(BF16)
    have = jnp.stack([own, xor(own, 0, 2)])
    bit = 2
    while bit < wide:
        got = have.astype(F32) + xor(have, bit, 0).astype(F32)
        if 2 * bit < wide:
            got = got + xor(have, 2 * bit, 0).astype(F32) + xor(have, 3 * bit, 0).astype(F32)
        have = got.astype(BF16)
        bit *= 4
    over = xor(have, 0, 1)

    near_list = jnp.transpose(near_src, (0, 2, 1))[0]
    far_list = jnp.transpose(far_src, (2, 0, 1))
    mid_list = jnp.transpose(mid_src, (1, 0, 2))
    raw = tuple(map(in_hbm, (near_list, near_count, far_list)))
    near_i, lf_i, c2, s2, nbo, lcr = pl.pallas_call(
        inner_kernel,
        in_specs=[hbm] * 3 + [vm] * 4 + [hbm] * 2,
        out_specs=[vm] * 6,
        out_shape=[shp(inside, w, v, t=F32), shp(inside, w, v, t=F32), shp(n + 1, v, 2 * w), shp(n, v, 2 * w),
                   shp(2 * REACH, slots, w, v), shp(REACH, fars, w, v)],
        scratch_shapes=[
            pltpu.SMEM((slots, n), jnp.int32), pltpu.SMEM((1, n), jnp.int32), pltpu.SMEM((fars, 1, n), jnp.int32),
            dma((3,)), dma((3,)),
        ],
        compiler_params=pltpu.CompilerParams(vmem_limit_bytes=12 << 20),
        cost_estimate=pl.CostEstimate(flops=60_000_000, bytes_accessed=6_000_000, transcendentals=0),
        name="inner",
    )(*raw, cp, sp, nbi, lci, in_hbm(near_blocks[0]), in_hbm(leaf_coupling[0]))
    near_o, lf_o = pl.pallas_call(
        outer_kernel,
        in_specs=[hbm] * 3 + [vm] * 7,
        out_specs=[vm] * 2,
        out_shape=[shp(2 * REACH, w, v, t=F32), shp(2 * REACH, w, v, t=F32)],
        scratch_shapes=[
            pltpu.VMEM((2 * REACH, fars, w, v), BF16),
            pltpu.VMEM((n + 2 * REACH + 1, v, 2 * w), BF16),
            pltpu.VMEM((n + 2 * REACH, v, 2 * w), BF16),
            pltpu.SMEM((slots, n), jnp.int32), pltpu.SMEM((1, n), jnp.int32), pltpu.SMEM((fars, 1, n), jnp.int32),
            dma((3,)), dma((4,)),
        ],
        compiler_params=pltpu.CompilerParams(vmem_limit_bytes=16 << 20),
        cost_estimate=pl.CostEstimate(flops=140_000_000, bytes_accessed=8_000_000, transcendentals=0),
        name="outer",
    )(*raw, c2, s2, f0, f1, nbo, lcl, lcr)
    mf = pl.pallas_call(
        middle_kernel,
        in_specs=[hbm] + [vm] * 4,
        out_specs=vm,
        out_shape=shp(mids, w, v, t=F32),
        scratch_shapes=[
            pltpu.VMEM((mids + 2 * MREACH, v, 2 * w), BF16), pltpu.SMEM((mids, 1, mfars), jnp.int32), dma((1,)),
        ],
        compiler_params=pltpu.CompilerParams(vmem_limit_bytes=8 << 20),
        cost_estimate=pl.CostEstimate(flops=20_000_000, bytes_accessed=3_000_000, transcendentals=0),
        name="middle",
    )(in_hbm(mid_list), mp, f0, f1, mc)

    out = pl.pallas_call(
        down_kernel,
        in_specs=[vm] * 12,
        out_specs=hbm,
        out_shape=shp(n, w, v),
        scratch_shapes=[pltpu.VMEM((n, w, v), BF16), dma((mids // 2,))],
        compiler_params=pltpu.CompilerParams(vmem_limit_bytes=16 << 20),
        cost_estimate=pl.CostEstimate(flops=30_000_000, bytes_accessed=4_000_000, transcendentals=0),
        name="down",
    )(have, over, top_coupling[0], down_top[0], down_mid[0], column_transfer_leaf[0], leaf_column_basis[0],
      near_i, lf_i, near_o, lf_o, mf)
    return out[None]


def solution(mesh):
    leaf = P("narrow", "wide", None, None)
    block = P("narrow", "wide", None, None, None)
    lists = P("narrow", "wide", None)
    return jax.shard_map(
        apply,
        mesh=mesh,
        in_specs=(
            leaf, leaf, leaf, block, lists, P("narrow", "wide"), block, lists,
            leaf, leaf, block, lists, leaf, leaf, leaf, leaf, P("narrow", None, None, None),
        ),
        out_specs=leaf,
        check_vma=False,
    )
```

```python
import jax
import jax.numpy as jnp
from jax import lax
from jax.experimental import pallas as pl
from jax.experimental.pallas import tpu as pltpu
from jax.sharding import PartitionSpec as P


REACH = 8
MREACH = 6
F32 = jnp.float32
BF16 = jnp.bfloat16
NN = (((1,), (0,)), ((), ()))
NT = (((1,), (1,)), ((), ()))


def nn(a, b):
    return lax.dot_general(a, b, NN, preferred_element_type=F32)


def nt(a, b):
    return lax.dot_general(a, b, NT, preferred_element_type=F32)


def beside(*parts):
    return jnp.concatenate(parts, axis=1)


def rows(ref, *at):
    x = ref[at]
    return x.reshape(-1, x.shape[-1])


def in_hbm(x):
    return pltpu.with_memory_space_constraint(x, pltpu.HBM)


def up_kernel(c_hbm, r_hbm, ul_hbm, um_hbm, ut_hbm, nb_hbm, lc_hbm,
              cp_ref, sp_ref, mp_ref, e0_ref, e1_ref, dt_ref, nbi_ref, lci_ref,
              c_ref, r_ref, ul_ref, um_ref, ut_ref, sems):
    n, w = c_ref.shape[:2]
    mids = um_ref.shape[0]
    copies = [
        pltpu.make_async_copy(src, dst, sems.at[j])
        for j, (src, dst) in enumerate(
            ((c_hbm, c_ref), (r_hbm, r_ref), (ul_hbm, ul_ref), (um_hbm, um_ref), (ut_hbm, ut_ref)))
    ]
    inside = pl.ds(REACH, nbi_ref.shape[0])
    later = [
        pltpu.make_async_copy(nb_hbm.at[inside], nbi_ref, sems.at[5]),
        pltpu.make_async_copy(lc_hbm.at[inside], lci_ref, sems.at[6]),
    ]
    for copy in copies + later:
        copy.start()
    eye = (
        lax.broadcasted_iota(jnp.int32, (w, w), 0) == lax.broadcasted_iota(jnp.int32, (w, w), 1)
    ).astype(F32).astype(BF16)
    zero = jnp.zeros((w, w), BF16)
    zeros = jnp.zeros((w, 2 * w), BF16)
    odd = lax.axis_index("wide") % 2
    copies[0].wait()
    cts = [nt(eye, rows(c_ref, pl.ds(4 * m, 4))).astype(BF16) for m in range(mids)]
    for copy in copies[1:]:
        copy.wait()
    top = nn(rows(um_ref, pl.ds(0, mids)), ut_ref[0]).astype(BF16)
    sts = []
    for m in range(mids):
        i = 4 * m
        blocks = jnp.concatenate([
            beside(beside(r_ref[i], zero), zeros),
            beside(beside(zero, r_ref[i + 1]), zeros),
            beside(zeros, beside(r_ref[i + 2], zero)),
            beside(zeros, beside(zero, r_ref[i + 3])),
        ], axis=0)
        sts.append(nn(cts[m], blocks).astype(BF16))
    for m in range(mids):
        cp_ref[2 * m] = cts[m][:, : 2 * w]
        cp_ref[2 * m + 1] = cts[m][:, 2 * w :]
        sp_ref[2 * m] = sts[m][:, : 2 * w]
        sp_ref[2 * m + 1] = sts[m][:, 2 * w :]
    mid = [nn(sts[m], rows(ul_ref, pl.ds(4 * m, 4))) for m in range(mids)]
    pairs = [beside(mid[2 * m], mid[2 * m + 1]).astype(BF16) for m in range(mids // 2)]
    for m in range(mids // 2):
        mp_ref[m] = pairs[m]
    term = nn(beside(*pairs), top)
    h = term.shape[0] // 2
    dt_ref[...] = beside(term[:h], term[h:]).astype(BF16)
    half, mhalf = REACH // 2, MREACH // 2
    for e_ref, right in ((e0_ref, 1 - odd), (e1_ref, odd)):
        at = right * (n // 2 - half)
        mat = right * (mids // 2 - mhalf)
        for k in range(half):
            e_ref[k] = cp_ref[at + k]
            e_ref[half + k] = sp_ref[at + k]
        for k in range(mhalf):
            e_ref[2 * half + k] = mp_ref[mat + k]
    for copy in later:
        copy.wait()


def both_ways(pair, tab, at):
    w = pair.shape[1] // 2
    tab[at] = pair
    tab[at + 1] = beside(pair[:, w:], pair[:, :w])


def low(w):
    return lax.broadcasted_iota(jnp.int32, (w, 2 * w), 1) < w


def side(lo, tab, idx):
    return beside(*[jnp.where(lo, tab[idx[k]], tab[idx[k + 1] ^ 1]) for k in range(0, len(idx), 2)])


def lists_in(near_hbm, count_hbm, far_hbm, ni_ref, nc_ref, fi_ref, sems):
    return [
        pltpu.make_async_copy(src, dst, sems.at[j])
        for j, (src, dst) in enumerate(((near_hbm, ni_ref), (count_hbm, nc_ref), (far_hbm, fi_ref)))
    ]


def inner_kernel(near_hbm, count_hbm, far_hbm, cp_ref, sp_ref, nb_ref, lc_ref, nb_hbm, lc_hbm,
                 near_ref, lf_ref, c2_ref, s2_ref, nbo_ref, lco_ref, ni_ref, nc_ref, fi_ref, small, big):
    slots, fars = nb_ref.shape[1], lc_ref.shape[1]
    n = s2_ref.shape[0]
    inside = near_ref.shape[0]
    right = pl.ds(n - REACH, REACH)
    later = [
        pltpu.make_async_copy(nb_hbm.at[pl.ds(0, REACH)], nbo_ref.at[pl.ds(0, REACH)], big.at[0]),
        pltpu.make_async_copy(nb_hbm.at[right], nbo_ref.at[pl.ds(REACH, REACH)], big.at[1]),
        pltpu.make_async_copy(lc_hbm.at[pl.ds(0, REACH)], lco_ref.at[pl.ds(0, REACH)], big.at[2]),
        pltpu.make_async_copy(lc_hbm.at[right], lco_ref.at[pl.ds(REACH, REACH)], big.at[3]),
    ]
    w = c2_ref.shape[1]
    lists = lists_in(near_hbm, count_hbm, far_hbm, ni_ref, nc_ref, fi_ref, small)
    for copy in lists + later:
        copy.start()
    lo = low(w)

    @pl.loop(0, n // 8)
    def _(g):
        for q in range(4):
            k = 4 * g + q
            both_ways(cp_ref[k], c2_ref, 2 * k)
            both_ways(sp_ref[k], s2_ref, 2 * k)

    for k in range(2):
        c2_ref[n + k] = jnp.zeros(c2_ref.shape[1:], BF16)
    base = lax.axis_index("wide") * n
    for copy in lists:
        copy.wait()

    @pl.loop(0, inside // 4)
    def _(g):
        for r in range(4):
            q = 4 * g + r
            i = REACH + q
            live = nc_ref[0, i]
            idx = [jnp.where(k < live, ni_ref[k, i] - base, n) for k in range(slots)]
            near_ref[q] = jnp.transpose(nn(side(lo, c2_ref, idx), rows(nb_ref, q)))
            idx = [fi_ref[k, 0, i] - base for k in range(fars)]
            lf_ref[q] = jnp.transpose(nn(side(lo, s2_ref, idx), rows(lc_ref, q)))

    for copy in later:
        copy.wait()


def outer_kernel(near_hbm, count_hbm, far_hbm, c2_ref, s2_ref, f0_ref, f1_ref, nb_ref, lc_ref,
                 near_ref, lf_ref, ctab, stab, ni_ref, nc_ref, fi_ref, small, big):
    slots, fars = nb_ref.shape[1], lc_ref.shape[1]
    n = c2_ref.shape[0] - 2
    w = c2_ref.shape[1]
    copies = lists_in(near_hbm, count_hbm, far_hbm, ni_ref, nc_ref, fi_ref, small) + [
        pltpu.make_async_copy(c2_ref.at[pl.ds(0, n)], ctab.at[pl.ds(REACH, n)], big.at[0]),
        pltpu.make_async_copy(s2_ref, stab.at[pl.ds(REACH, n)], big.at[1]),
    ]
    for copy in copies:
        copy.start()
    lo = low(w)
    pos = lax.axis_index("wide")
    odd = pos % 2
    half = REACH // 2
    for f_ref, right in ((f0_ref, 1 - odd), (f1_ref, odd)):
        at = right * (n + REACH)
        for k in range(half):
            both_ways(f_ref[k], ctab, at + 2 * k)
            both_ways(f_ref[half + k], stab, at + 2 * k)
    for k in range(2):
        ctab[n + 2 * REACH + k] = jnp.zeros(ctab.shape[1:], BF16)
    base = pos * n - REACH
    for copy in copies:
        copy.wait()

    @pl.loop(0, 2)
    def _(g):
        for q in range(REACH):
            j = g * REACH + q
            i = g * (n - REACH) + q
            live = nc_ref[0, i]
            idx = [jnp.where(k < live, ni_ref[k, i] - base, n + 2 * REACH) for k in range(slots)]
            near_ref[j] = jnp.transpose(nn(side(lo, ctab, idx), rows(nb_ref, j)))
            idx = [fi_ref[k, 0, i] - base for k in range(fars)]
            lf_ref[j] = jnp.transpose(nn(side(lo, stab, idx), rows(lc_ref, j)))


def middle_kernel(mid_hbm, mp_ref, f0_ref, f1_ref, mc_ref, dm_ref, dtop_ref, mf_ref, both_ref, mtab, mi_ref, small):
    mids, mfars = mc_ref.shape[:2]
    w = mtab.shape[1]
    copy = pltpu.make_async_copy(mid_hbm, mi_ref, small.at[0])
    copy.start()
    lo = low(w)
    pos = lax.axis_index("wide")
    odd = pos % 2
    for k in range(mids // 2):
        both_ways(mp_ref[k], mtab, MREACH + 2 * k)
    for f_ref, right in ((f0_ref, 1 - odd), (f1_ref, odd)):
        for k in range(MREACH // 2):
            both_ways(f_ref[REACH + k], mtab, right * (mids + MREACH) + 2 * k)
    both_ref[...] = nn(rows(dm_ref, pl.ds(0, mids)), dtop_ref[0]).astype(BF16)
    base = pos * mids - MREACH
    copy.wait()
    for j in range(mids):
        idx = [mi_ref[j, 0, k] - base for k in range(mfars)]
        mf_ref[j] = jnp.transpose(nn(side(lo, mtab, idx), rows(mc_ref, j)))


def down_kernel(own_ref, over_ref, tc_ref, both_ref, tl_ref, cb_ref, neari_ref, lfi_ref, nearo_ref, lfo_ref, mf_ref,
                out_hbm, out_ref, sems):
    mids = mf_ref.shape[0]
    n = tl_ref.shape[0]
    me = lax.axis_index("narrow")
    acc = None
    for ref, k, h in ((own_ref, 1, me ^ 2), (over_ref, 0, me ^ 1), (over_ref, 1, me ^ 3)):
        g = ref[k]
        c = g.shape[1] // 2
        gt = jnp.concatenate([g[:, :c], g[:, c:]], axis=0)
        part = nn(gt, tc_ref[h])
        acc = part if acc is None else acc + part
    down = nt(both_ref[...], acc.astype(BF16))
    r = tl_ref.shape[1]
    copies = []
    for m in range(mids):
        md = (mf_ref[m] + down[m * r : (m + 1) * r]).astype(BF16)
        ld = nn(rows(tl_ref, pl.ds(4 * m, 4)), md)
        for q in range(4):
            i = 4 * m + q
            if REACH <= i < n - REACH:
                near, lf = neari_ref[i - REACH], lfi_ref[i - REACH]
            else:
                j = i if i < REACH else i - (n - 2 * REACH)
                near, lf = nearo_ref[j], lfo_ref[j]
            lq = (lf + ld[q * r : (q + 1) * r]).astype(BF16)
            out_ref[i] = (near + nn(cb_ref[i], lq)).astype(BF16)
        if m % 2 == 1:
            part = pl.ds(4 * (m - 1), 8)
            copy = pltpu.make_async_copy(out_ref.at[part], out_hbm.at[part], sems.at[m // 2])
            copy.start()
            copies.append(copy)
    for copy in copies:
        copy.wait()


def apply(
    charges, leaf_row_basis, leaf_column_basis, near_blocks, near_src, near_count, leaf_coupling, far_src,
    up_leaf, column_transfer_leaf, mid_coupling, mid_src, up_mid, down_mid, up_top, down_top, top_coupling,
):
    n, w, v = charges.shape[1:]
    mids = up_mid.shape[1]
    wide, narrow = lax.axis_size("wide"), lax.axis_size("narrow")
    both = ("wide", "narrow")
    pairs = REACH + MREACH // 2
    slots, fars, mfars = near_src.shape[2], far_src.shape[2], mid_src.shape[2]
    hbm = pl.BlockSpec(memory_space=pltpu.HBM)
    vm = pl.BlockSpec(memory_space=pltpu.VMEM)
    dma = pltpu.SemaphoreType.DMA

    def shp(*s, t=BF16):
        return jax.ShapeDtypeStruct(s, t)

    inside = n - 2 * REACH
    cp, sp, mp, e0, e1, term, nbi, lci = pl.pallas_call(
        up_kernel,
        in_specs=[hbm] * 7,
        out_specs=[vm] * 8,
        out_shape=[shp(n // 2, v, 2 * w), shp(n // 2, v, 2 * w), shp(mids // 2, v, 2 * w),
                   shp(pairs, v, 2 * w), shp(pairs, v, 2 * w), shp(v // 2, 2 * w),
                   shp(inside, slots, w, v), shp(inside, fars, w, v)],
        scratch_shapes=[
            pltpu.VMEM((n, w, v), BF16), pltpu.VMEM((n, w, v), BF16), pltpu.VMEM((n, w, v), BF16),
            pltpu.VMEM((mids, w, v), BF16), pltpu.VMEM((1, w, v), BF16), dma((7,)),
        ],
        compiler_params=pltpu.CompilerParams(vmem_limit_bytes=16 << 20),
        cost_estimate=pl.CostEstimate(flops=30_000_000, bytes_accessed=4_000_000, transcendentals=0),
        name="up",
    )(*map(in_hbm, (charges[0], leaf_row_basis[0], up_leaf[0], up_mid[0], up_top[0],
                  near_blocks[0], leaf_coupling[0])))

    def xor(x, dw, dn):
        return lax.ppermute(x, both, [(i * narrow + j, (i ^ dw) * narrow + (j ^ dn)) for i in range(wide) for j in range(narrow)])

    f0 = lax.ppermute(e0, "wide", [(i, i ^ 1) for i in range(wide)])
    f1 = lax.ppermute(e1, "wide", [(i, (((i + 1) ^ 1) - 1) % wide) for i in range(wide)])
    f = term.astype(F32)
    own = (f + xor(term, 1, 0).astype(F32)).astype(BF16)
    have = jnp.stack([own, xor(own, 0, 2)])
    bit = 2
    while bit < wide:
        got = have.astype(F32) + xor(have, bit, 0).astype(F32)
        if 2 * bit < wide:
            got = got + xor(have, 2 * bit, 0).astype(F32) + xor(have, 3 * bit, 0).astype(F32)
        have = got.astype(BF16)
        bit *= 4
    over = xor(have, 0, 1)

    near_list = jnp.transpose(near_src, (0, 2, 1))[0]
    far_list = jnp.transpose(far_src, (2, 0, 1))
    mid_list = jnp.transpose(mid_src, (1, 0, 2))
    raw = tuple(map(in_hbm, (near_list, near_count, far_list)))
    near_i, lf_i, c2, s2, nbo, lco = pl.pallas_call(
        inner_kernel,
        in_specs=[hbm] * 3 + [vm] * 4 + [hbm] * 2,
        out_specs=[vm] * 6,
        out_shape=[shp(inside, w, v, t=F32), shp(inside, w, v, t=F32), shp(n + 2, v, 2 * w), shp(n, v, 2 * w),
                   shp(2 * REACH, slots, w, v), shp(2 * REACH, fars, w, v)],
        scratch_shapes=[
            pltpu.SMEM((slots, n), jnp.int32), pltpu.SMEM((1, n), jnp.int32), pltpu.SMEM((fars, 1, n), jnp.int32),
            dma((3,)), dma((4,)),
        ],
        compiler_params=pltpu.CompilerParams(vmem_limit_bytes=12 << 20),
        cost_estimate=pl.CostEstimate(flops=60_000_000, bytes_accessed=6_000_000, transcendentals=0),
        name="inner",
    )(*raw, cp, sp, nbi, lci, in_hbm(near_blocks[0]), in_hbm(leaf_coupling[0]))
    near_o, lf_o = pl.pallas_call(
        outer_kernel,
        in_specs=[hbm] * 3 + [vm] * 6,
        out_specs=[vm] * 2,
        out_shape=[shp(2 * REACH, w, v, t=F32), shp(2 * REACH, w, v, t=F32)],
        scratch_shapes=[
            pltpu.VMEM((n + 2 * REACH + 2, v, 2 * w), BF16),
            pltpu.VMEM((n + 2 * REACH, v, 2 * w), BF16),
            pltpu.SMEM((slots, n), jnp.int32), pltpu.SMEM((1, n), jnp.int32), pltpu.SMEM((fars, 1, n), jnp.int32),
            dma((3,)), dma((4,)),
        ],
        compiler_params=pltpu.CompilerParams(vmem_limit_bytes=16 << 20),
        cost_estimate=pl.CostEstimate(flops=140_000_000, bytes_accessed=8_000_000, transcendentals=0),
        name="outer",
    )(*raw, c2, s2, f0, f1, nbo, lco)
    mf, down_both = pl.pallas_call(
        middle_kernel,
        in_specs=[hbm] + [vm] * 6,
        out_specs=[vm] * 2,
        out_shape=[shp(mids, w, v, t=F32), shp(mids * w, w)],
        scratch_shapes=[
            pltpu.VMEM((mids + 2 * MREACH, v, 2 * w), BF16), pltpu.SMEM((mids, 1, mfars), jnp.int32), dma((1,)),
        ],
        compiler_params=pltpu.CompilerParams(vmem_limit_bytes=8 << 20),
        cost_estimate=pl.CostEstimate(flops=20_000_000, bytes_accessed=3_000_000, transcendentals=0),
        name="middle",
    )(in_hbm(mid_list), mp, f0, f1, mid_coupling[0], down_mid[0], down_top[0])

    out = pl.pallas_call(
        down_kernel,
        in_specs=[vm] * 11,
        out_specs=hbm,
        out_shape=shp(n, w, v),
        scratch_shapes=[pltpu.VMEM((n, w, v), BF16), dma((mids // 2,))],
        compiler_params=pltpu.CompilerParams(vmem_limit_bytes=16 << 20),
        cost_estimate=pl.CostEstimate(flops=30_000_000, bytes_accessed=4_000_000, transcendentals=0),
        name="down",
    )(have, over, top_coupling[0], down_both, column_transfer_leaf[0], leaf_column_basis[0],
      near_i, lf_i, near_o, lf_o, mf)
    return out[None]


def solution(mesh):
    leaf = P("narrow", "wide", None, None)
    block = P("narrow", "wide", None, None, None)
    lists = P("narrow", "wide", None)
    return jax.shard_map(
        apply,
        mesh=mesh,
        in_specs=(
            leaf, leaf, leaf, block, lists, P("narrow", "wide"), block, lists,
            leaf, leaf, block, lists, leaf, leaf, leaf, leaf, P("narrow", None, None, None),
        ),
        out_specs=leaf,
        check_vma=False,
    )
```

```python
import jax
import jax.numpy as jnp
from jax import lax
from jax.experimental import pallas as pl
from jax.experimental.pallas import tpu as pltpu
from jax.sharding import PartitionSpec as P


REACH = 8
MREACH = 6
F32 = jnp.float32
BF16 = jnp.bfloat16
NN = (((1,), (0,)), ((), ()))
NT = (((1,), (1,)), ((), ()))


def nn(a, b):
    return lax.dot_general(a, b, NN, preferred_element_type=F32)


def nt(a, b):
    return lax.dot_general(a, b, NT, preferred_element_type=F32)


def beside(*parts):
    return jnp.concatenate(parts, axis=1)


def rows(ref, *at):
    x = ref[at]
    return x.reshape(-1, x.shape[-1])


def in_hbm(x):
    return pltpu.with_memory_space_constraint(x, pltpu.HBM)


def up_kernel(c_hbm, r_hbm, ul_hbm, um_hbm, ut_hbm, nb_hbm, lc_hbm,
              cp_ref, sp_ref, mp_ref, e0_ref, e1_ref, dt_ref, nbi_ref, lci_ref,
              c_ref, r_ref, ul_ref, um_ref, ut_ref, sems):
    n, w = c_ref.shape[:2]
    mids = um_ref.shape[0]
    copies = [
        pltpu.make_async_copy(src, dst, sems.at[j])
        for j, (src, dst) in enumerate(
            ((c_hbm, c_ref), (r_hbm, r_ref), (ul_hbm, ul_ref), (um_hbm, um_ref), (ut_hbm, ut_ref)))
    ]
    inside = pl.ds(REACH, nbi_ref.shape[0])
    later = [
        pltpu.make_async_copy(nb_hbm.at[inside], nbi_ref, sems.at[5]),
        pltpu.make_async_copy(lc_hbm.at[inside], lci_ref, sems.at[6]),
    ]
    for copy in copies + later:
        copy.start()
    eye = (
        lax.broadcasted_iota(jnp.int32, (w, w), 0) == lax.broadcasted_iota(jnp.int32, (w, w), 1)
    ).astype(F32).astype(BF16)
    zero = jnp.zeros((w, w), BF16)
    zeros = jnp.zeros((w, 2 * w), BF16)
    odd = lax.axis_index("wide") % 2
    copies[0].wait()
    cts = [nt(eye, rows(c_ref, pl.ds(4 * m, 4))).astype(BF16) for m in range(mids)]
    for copy in copies[1:]:
        copy.wait()
    top = nn(rows(um_ref, pl.ds(0, mids)), ut_ref[0]).astype(BF16)
    sts = []
    for m in range(mids):
        i = 4 * m
        blocks = jnp.concatenate([
            beside(beside(r_ref[i], zero), zeros),
            beside(beside(zero, r_ref[i + 1]), zeros),
            beside(zeros, beside(r_ref[i + 2], zero)),
            beside(zeros, beside(zero, r_ref[i + 3])),
        ], axis=0)
        sts.append(nn(cts[m], blocks).astype(BF16))
    for m in range(mids):
        cp_ref[2 * m] = cts[m][:, : 2 * w]
        cp_ref[2 * m + 1] = cts[m][:, 2 * w :]
        sp_ref[2 * m] = sts[m][:, : 2 * w]
        sp_ref[2 * m + 1] = sts[m][:, 2 * w :]
    mid = [nn(sts[m], rows(ul_ref, pl.ds(4 * m, 4))) for m in range(mids)]
    pairs = [beside(mid[2 * m], mid[2 * m + 1]).astype(BF16) for m in range(mids // 2)]
    for m in range(mids // 2):
        mp_ref[m] = pairs[m]
    term = nn(beside(*pairs), top)
    h = term.shape[0] // 2
    dt_ref[...] = beside(term[:h], term[h:]).astype(BF16)
    half, mhalf = REACH // 2, MREACH // 2
    for e_ref, right in ((e0_ref, 1 - odd), (e1_ref, odd)):
        at = right * (n // 2 - half)
        mat = right * (mids // 2 - mhalf)
        for k in range(half):
            e_ref[k] = cp_ref[at + k]
            e_ref[half + k] = sp_ref[at + k]
        for k in range(mhalf):
            e_ref[2 * half + k] = mp_ref[mat + k]
    for copy in later:
        copy.wait()


def both_ways(pair, tab, at):
    w = pair.shape[1] // 2
    tab[at] = pair
    tab[at + 1] = beside(pair[:, w:], pair[:, :w])


def low(w):
    return lax.broadcasted_iota(jnp.int32, (w, 2 * w), 1) < w


def side(lo, tab, idx):
    return beside(*[jnp.where(lo, tab[idx[k]], tab[idx[k + 1] ^ 1]) for k in range(0, len(idx), 2)])


def lists_in(near_hbm, count_hbm, far_hbm, ni_ref, nc_ref, fi_ref, sems):
    return [
        pltpu.make_async_copy(src, dst, sems.at[j])
        for j, (src, dst) in enumerate(((near_hbm, ni_ref), (count_hbm, nc_ref), (far_hbm, fi_ref)))
    ]


def inner_kernel(near_hbm, count_hbm, far_hbm, cp_ref, sp_ref, nb_ref, lc_ref, nb_hbm, lc_hbm,
                 near_ref, lf_ref, c2_ref, s2_ref, nbo_ref, lco_ref, ni_ref, nc_ref, fi_ref, small, big):
    slots, fars = nb_ref.shape[1], lc_ref.shape[1]
    n = s2_ref.shape[0]
    inside = near_ref.shape[0]
    right = pl.ds(n - REACH, REACH)
    later = [
        pltpu.make_async_copy(nb_hbm.at[pl.ds(0, REACH)], nbo_ref.at[pl.ds(0, REACH)], big.at[0]),
        pltpu.make_async_copy(nb_hbm.at[right], nbo_ref.at[pl.ds(REACH, REACH)], big.at[1]),
        pltpu.make_async_copy(lc_hbm.at[pl.ds(0, REACH)], lco_ref.at[pl.ds(0, REACH)], big.at[2]),
        pltpu.make_async_copy(lc_hbm.at[right], lco_ref.at[pl.ds(REACH, REACH)], big.at[3]),
    ]
    w = c2_ref.shape[1]
    lists = lists_in(near_hbm, count_hbm, far_hbm, ni_ref, nc_ref, fi_ref, small)
    for copy in lists + later:
        copy.start()
    lo = low(w)

    @pl.loop(0, n // 8)
    def _(g):
        for q in range(4):
            k = 4 * g + q
            both_ways(cp_ref[k], c2_ref, 2 * k)
            both_ways(sp_ref[k], s2_ref, 2 * k)

    for k in range(2):
        c2_ref[n + k] = jnp.zeros(c2_ref.shape[1:], BF16)
    base = lax.axis_index("wide") * n
    for copy in lists:
        copy.wait()

    @pl.loop(0, inside // 4)
    def _(g):
        for r in range(4):
            q = 4 * g + r
            i = REACH + q
            live = nc_ref[0, i]
            idx = [jnp.where(k < live, ni_ref[k, i] - base, n) for k in range(slots)]
            near_ref[q] = jnp.transpose(nn(side(lo, c2_ref, idx), rows(nb_ref, q)))
            idx = [fi_ref[k, 0, i] - base for k in range(fars)]
            lf_ref[q] = jnp.transpose(nn(side(lo, s2_ref, idx), rows(lc_ref, q)))

    for copy in later:
        copy.wait()


def outer_kernel(near_hbm, count_hbm, far_hbm, c2_ref, s2_ref, f0_ref, f1_ref, nb_ref, lc_ref,
                 near_ref, lf_ref, ctab, stab, ni_ref, nc_ref, fi_ref, small, big):
    slots, fars = nb_ref.shape[1], lc_ref.shape[1]
    n = c2_ref.shape[0] - 2
    w = c2_ref.shape[1]
    copies = lists_in(near_hbm, count_hbm, far_hbm, ni_ref, nc_ref, fi_ref, small) + [
        pltpu.make_async_copy(c2_ref.at[pl.ds(0, n)], ctab.at[pl.ds(REACH, n)], big.at[0]),
        pltpu.make_async_copy(s2_ref, stab.at[pl.ds(REACH, n)], big.at[1]),
    ]
    for copy in copies:
        copy.start()
    lo = low(w)
    pos = lax.axis_index("wide")
    odd = pos % 2
    half = REACH // 2
    for f_ref, right in ((f0_ref, 1 - odd), (f1_ref, odd)):
        at = right * (n + REACH)
        for k in range(half):
            both_ways(f_ref[k], ctab, at + 2 * k)
            both_ways(f_ref[half + k], stab, at + 2 * k)
    for k in range(2):
        ctab[n + 2 * REACH + k] = jnp.zeros(ctab.shape[1:], BF16)
    base = pos * n - REACH
    for copy in copies:
        copy.wait()

    @pl.loop(0, 2)
    def _(g):
        for q in range(REACH):
            j = g * REACH + q
            i = g * (n - REACH) + q
            live = nc_ref[0, i]
            idx = [jnp.where(k < live, ni_ref[k, i] - base, n + 2 * REACH) for k in range(slots)]
            near_ref[j] = jnp.transpose(nn(side(lo, ctab, idx), rows(nb_ref, j)))
            idx = [fi_ref[k, 0, i] - base for k in range(fars)]
            lf_ref[j] = jnp.transpose(nn(side(lo, stab, idx), rows(lc_ref, j)))


def middle_kernel(mid_hbm, mp_ref, f0_ref, f1_ref, mc_ref, dm_ref, dtop_ref, mf_ref, both_ref, mtab, mi_ref, small):
    mids, mfars = mc_ref.shape[:2]
    w = mtab.shape[1]
    copy = pltpu.make_async_copy(mid_hbm, mi_ref, small.at[0])
    copy.start()
    lo = low(w)
    pos = lax.axis_index("wide")
    odd = pos % 2
    for k in range(mids // 2):
        both_ways(mp_ref[k], mtab, MREACH + 2 * k)
    for f_ref, right in ((f0_ref, 1 - odd), (f1_ref, odd)):
        for k in range(MREACH // 2):
            both_ways(f_ref[REACH + k], mtab, right * (mids + MREACH) + 2 * k)
    both_ref[...] = nn(rows(dm_ref, pl.ds(0, mids)), dtop_ref[0]).astype(BF16)
    base = pos * mids - MREACH
    copy.wait()
    for j in range(mids):
        idx = [mi_ref[j, 0, k] - base for k in range(mfars)]
        mf_ref[j] = jnp.transpose(nn(side(lo, mtab, idx), rows(mc_ref, j)))


def down_kernel(own_ref, over_ref, tc_ref, both_ref, tl_ref, cb_ref, neari_ref, lfi_ref, nearo_ref, lfo_ref, mf_ref,
                out_hbm, out_ref, sems):
    mids = mf_ref.shape[0]
    n = tl_ref.shape[0]
    me = lax.axis_index("narrow")
    acc = None
    for ref, k, h in ((own_ref, 1, me ^ 2), (over_ref, 0, me ^ 1), (over_ref, 1, me ^ 3)):
        g = ref[k]
        c = g.shape[1] // 2
        gt = jnp.concatenate([g[:, :c], g[:, c:]], axis=0)
        part = nn(gt, tc_ref[h])
        acc = part if acc is None else acc + part
    down = nt(both_ref[...], acc.astype(BF16))
    r = tl_ref.shape[1]
    copies = []
    for m in range(mids):
        md = (mf_ref[m] + down[m * r : (m + 1) * r]).astype(BF16)
        ld = nn(rows(tl_ref, pl.ds(4 * m, 4)), md)
        for q in range(4):
            i = 4 * m + q
            if REACH <= i < n - REACH:
                near, lf = neari_ref[i - REACH], lfi_ref[i - REACH]
            else:
                j = i if i < REACH else i - (n - 2 * REACH)
                near, lf = nearo_ref[j], lfo_ref[j]
            lq = (lf + ld[q * r : (q + 1) * r]).astype(BF16)
            out_ref[i] = (near + nn(cb_ref[i], lq)).astype(BF16)
        part = pl.ds(4 * m, 4)
        copy = pltpu.make_async_copy(out_ref.at[part], out_hbm.at[part], sems.at[m])
        copy.start()
        copies.append(copy)
    for copy in copies:
        copy.wait()


def apply(
    charges, leaf_row_basis, leaf_column_basis, near_blocks, near_src, near_count, leaf_coupling, far_src,
    up_leaf, column_transfer_leaf, mid_coupling, mid_src, up_mid, down_mid, up_top, down_top, top_coupling,
):
    n, w, v = charges.shape[1:]
    mids = up_mid.shape[1]
    wide, narrow = lax.axis_size("wide"), lax.axis_size("narrow")
    both = ("wide", "narrow")
    pairs = REACH + MREACH // 2
    slots, fars, mfars = near_src.shape[2], far_src.shape[2], mid_src.shape[2]
    hbm = pl.BlockSpec(memory_space=pltpu.HBM)
    vm = pl.BlockSpec(memory_space=pltpu.VMEM)
    dma = pltpu.SemaphoreType.DMA

    def shp(*s, t=BF16):
        return jax.ShapeDtypeStruct(s, t)

    inside = n - 2 * REACH
    cp, sp, mp, e0, e1, term, nbi, lci = pl.pallas_call(
        up_kernel,
        in_specs=[hbm] * 7,
        out_specs=[vm] * 8,
        out_shape=[shp(n // 2, v, 2 * w), shp(n // 2, v, 2 * w), shp(mids // 2, v, 2 * w),
                   shp(pairs, v, 2 * w), shp(pairs, v, 2 * w), shp(v // 2, 2 * w),
                   shp(inside, slots, w, v), shp(inside, fars, w, v)],
        scratch_shapes=[
            pltpu.VMEM((n, w, v), BF16), pltpu.VMEM((n, w, v), BF16), pltpu.VMEM((n, w, v), BF16),
            pltpu.VMEM((mids, w, v), BF16), pltpu.VMEM((1, w, v), BF16), dma((7,)),
        ],
        compiler_params=pltpu.CompilerParams(vmem_limit_bytes=16 << 20),
        cost_estimate=pl.CostEstimate(flops=30_000_000, bytes_accessed=4_000_000, transcendentals=0),
        name="up",
    )(*map(in_hbm, (charges[0], leaf_row_basis[0], up_leaf[0], up_mid[0], up_top[0],
                  near_blocks[0], leaf_coupling[0])))

    def xor(x, dw, dn):
        return lax.ppermute(x, both, [(i * narrow + j, (i ^ dw) * narrow + (j ^ dn)) for i in range(wide) for j in range(narrow)])

    f0 = lax.ppermute(e0, "wide", [(i, i ^ 1) for i in range(wide)])
    ends = (0, wide - 1)
    f1 = lax.ppermute(e1, both, [
        (i * narrow + j, i * narrow + (j ^ 1) if i in ends else (((i + 1) ^ 1) - 1) * narrow + j)
        for i in range(wide) for j in range(narrow)
    ])
    f = term.astype(F32)
    own = (f + xor(term, 1, 0).astype(F32)).astype(BF16)
    have = jnp.stack([own, xor(own, 0, 2)])
    bit = 2
    while bit < wide:
        got = have.astype(F32) + xor(have, bit, 0).astype(F32)
        if 2 * bit < wide:
            got = got + xor(have, 2 * bit, 0).astype(F32) + xor(have, 3 * bit, 0).astype(F32)
        have = got.astype(BF16)
        bit *= 4
    over = xor(have, 0, 1)

    near_list = jnp.transpose(near_src, (0, 2, 1))[0]
    far_list = jnp.transpose(far_src, (2, 0, 1))
    mid_list = jnp.transpose(mid_src, (1, 0, 2))
    raw = tuple(map(in_hbm, (near_list, near_count, far_list)))
    near_i, lf_i, c2, s2, nbo, lco = pl.pallas_call(
        inner_kernel,
        in_specs=[hbm] * 3 + [vm] * 4 + [hbm] * 2,
        out_specs=[vm] * 6,
        out_shape=[shp(inside, w, v, t=F32), shp(inside, w, v, t=F32), shp(n + 2, v, 2 * w), shp(n, v, 2 * w),
                   shp(2 * REACH, slots, w, v), shp(2 * REACH, fars, w, v)],
        scratch_shapes=[
            pltpu.SMEM((slots, n), jnp.int32), pltpu.SMEM((1, n), jnp.int32), pltpu.SMEM((fars, 1, n), jnp.int32),
            dma((3,)), dma((4,)),
        ],
        compiler_params=pltpu.CompilerParams(vmem_limit_bytes=12 << 20),
        cost_estimate=pl.CostEstimate(flops=60_000_000, bytes_accessed=6_000_000, transcendentals=0),
        name="inner",
    )(*raw, cp, sp, nbi, lci, in_hbm(near_blocks[0]), in_hbm(leaf_coupling[0]))
    near_o, lf_o = pl.pallas_call(
        outer_kernel,
        in_specs=[hbm] * 3 + [vm] * 6,
        out_specs=[vm] * 2,
        out_shape=[shp(2 * REACH, w, v, t=F32), shp(2 * REACH, w, v, t=F32)],
        scratch_shapes=[
            pltpu.VMEM((n + 2 * REACH + 2, v, 2 * w), BF16),
            pltpu.VMEM((n + 2 * REACH, v, 2 * w), BF16),
            pltpu.SMEM((slots, n), jnp.int32), pltpu.SMEM((1, n), jnp.int32), pltpu.SMEM((fars, 1, n), jnp.int32),
            dma((3,)), dma((4,)),
        ],
        compiler_params=pltpu.CompilerParams(vmem_limit_bytes=16 << 20),
        cost_estimate=pl.CostEstimate(flops=140_000_000, bytes_accessed=8_000_000, transcendentals=0),
        name="outer",
    )(*raw, c2, s2, f0, f1, nbo, lco)
    mf, down_both = pl.pallas_call(
        middle_kernel,
        in_specs=[hbm] + [vm] * 6,
        out_specs=[vm] * 2,
        out_shape=[shp(mids, w, v, t=F32), shp(mids * w, w)],
        scratch_shapes=[
            pltpu.VMEM((mids + 2 * MREACH, v, 2 * w), BF16), pltpu.SMEM((mids, 1, mfars), jnp.int32), dma((1,)),
        ],
        compiler_params=pltpu.CompilerParams(vmem_limit_bytes=8 << 20),
        cost_estimate=pl.CostEstimate(flops=20_000_000, bytes_accessed=3_000_000, transcendentals=0),
        name="middle",
    )(in_hbm(mid_list), mp, f0, f1, mid_coupling[0], down_mid[0], down_top[0])

    out = pl.pallas_call(
        down_kernel,
        in_specs=[vm] * 11,
        out_specs=hbm,
        out_shape=shp(n, w, v),
        scratch_shapes=[pltpu.VMEM((n, w, v), BF16), dma((mids,))],
        compiler_params=pltpu.CompilerParams(vmem_limit_bytes=16 << 20),
        cost_estimate=pl.CostEstimate(flops=30_000_000, bytes_accessed=4_000_000, transcendentals=0),
        name="down",
    )(have, over, top_coupling[0], down_both, column_transfer_leaf[0], leaf_column_basis[0],
      near_i, lf_i, near_o, lf_o, mf)
    return out[None]


def solution(mesh):
    leaf = P("narrow", "wide", None, None)
    block = P("narrow", "wide", None, None, None)
    lists = P("narrow", "wide", None)
    return jax.shard_map(
        apply,
        mesh=mesh,
        in_specs=(
            leaf, leaf, leaf, block, lists, P("narrow", "wide"), block, lists,
            leaf, leaf, block, lists, leaf, leaf, leaf, leaf, P("narrow", None, None, None),
        ),
        out_specs=leaf,
        check_vma=False,
    )
```

```python
import jax
import jax.numpy as jnp
from jax import lax
from jax.experimental import pallas as pl
from jax.experimental.pallas import tpu as pltpu
from jax.sharding import PartitionSpec as P


REACH = 8
MREACH = 6
F32 = jnp.float32
BF16 = jnp.bfloat16
NN = (((1,), (0,)), ((), ()))
NT = (((1,), (1,)), ((), ()))


def nn(a, b):
    return lax.dot_general(a, b, NN, preferred_element_type=F32)


def nt(a, b):
    return lax.dot_general(a, b, NT, preferred_element_type=F32)


def beside(*parts):
    return jnp.concatenate(parts, axis=1)


def rows(ref, *at):
    x = ref[at]
    return x.reshape(-1, x.shape[-1])


def in_hbm(x):
    return pltpu.with_memory_space_constraint(x, pltpu.HBM)


def up_kernel(c_hbm, r_hbm, ul_hbm, um_hbm, ut_hbm, nb_hbm, lc_hbm,
              cp_ref, sp_ref, mp_ref, e0_ref, e1_ref, dt_ref, nbi_ref, lci_ref,
              c_ref, r_ref, ul_ref, um_ref, ut_ref, sems):
    n, w = c_ref.shape[:2]
    mids = um_ref.shape[0]
    copies = [
        pltpu.make_async_copy(src, dst, sems.at[j])
        for j, (src, dst) in enumerate(
            ((c_hbm, c_ref), (r_hbm, r_ref), (ul_hbm, ul_ref), (um_hbm, um_ref), (ut_hbm, ut_ref)))
    ]
    inside = pl.ds(REACH, nbi_ref.shape[0])
    later = [
        pltpu.make_async_copy(nb_hbm.at[inside], nbi_ref, sems.at[5]),
        pltpu.make_async_copy(lc_hbm.at[inside], lci_ref, sems.at[6]),
    ]
    for copy in copies + later:
        copy.start()
    eye = (
        lax.broadcasted_iota(jnp.int32, (w, w), 0) == lax.broadcasted_iota(jnp.int32, (w, w), 1)
    ).astype(F32).astype(BF16)
    zero = jnp.zeros((w, w), BF16)
    zeros = jnp.zeros((w, 2 * w), BF16)
    odd = lax.axis_index("wide") % 2
    copies[0].wait()
    cts = [nt(eye, rows(c_ref, pl.ds(4 * m, 4))).astype(BF16) for m in range(mids)]
    for copy in copies[1:]:
        copy.wait()
    top = nn(rows(um_ref, pl.ds(0, mids)), ut_ref[0]).astype(BF16)
    sts = []
    for m in range(mids):
        i = 4 * m
        blocks = jnp.concatenate([
            beside(beside(r_ref[i], zero), zeros),
            beside(beside(zero, r_ref[i + 1]), zeros),
            beside(zeros, beside(r_ref[i + 2], zero)),
            beside(zeros, beside(zero, r_ref[i + 3])),
        ], axis=0)
        sts.append(nn(cts[m], blocks).astype(BF16))
    for m in range(mids):
        cp_ref[2 * m] = cts[m][:, : 2 * w]
        cp_ref[2 * m + 1] = cts[m][:, 2 * w :]
        sp_ref[2 * m] = sts[m][:, : 2 * w]
        sp_ref[2 * m + 1] = sts[m][:, 2 * w :]
    mid = [nn(sts[m], rows(ul_ref, pl.ds(4 * m, 4))) for m in range(mids)]
    pairs = [beside(mid[2 * m], mid[2 * m + 1]).astype(BF16) for m in range(mids // 2)]
    for m in range(mids // 2):
        mp_ref[m] = pairs[m]
    term = nn(beside(*pairs), top)
    dt_ref[...] = term.astype(BF16)
    half, mhalf = REACH // 2, MREACH // 2
    for e_ref, right in ((e0_ref, 1 - odd), (e1_ref, odd)):
        at = right * (n // 2 - half)
        mat = right * (mids // 2 - mhalf)
        for k in range(half):
            e_ref[k] = cp_ref[at + k]
            e_ref[half + k] = sp_ref[at + k]
        for k in range(mhalf):
            e_ref[2 * half + k] = mp_ref[mat + k]
    for copy in later:
        copy.wait()


def both_ways(pair, tab, at):
    w = pair.shape[1] // 2
    tab[at] = pair
    tab[at + 1] = beside(pair[:, w:], pair[:, :w])


def low(w):
    return lax.broadcasted_iota(jnp.int32, (w, 2 * w), 1) < w


def side(lo, tab, idx):
    return beside(*[jnp.where(lo, tab[idx[k]], tab[idx[k + 1] ^ 1]) for k in range(0, len(idx), 2)])


def lists_in(near_hbm, count_hbm, far_hbm, ni_ref, nc_ref, fi_ref, sems):
    return [
        pltpu.make_async_copy(src, dst, sems.at[j])
        for j, (src, dst) in enumerate(((near_hbm, ni_ref), (count_hbm, nc_ref), (far_hbm, fi_ref)))
    ]


def inner_kernel(near_hbm, count_hbm, far_hbm, cp_ref, sp_ref, nb_ref, lc_ref, nb_hbm, lc_hbm,
                 near_ref, lf_ref, c2_ref, s2_ref, nbo_ref, lco_ref, ni_ref, nc_ref, fi_ref, small, big):
    slots, fars = nb_ref.shape[1], lc_ref.shape[1]
    n = s2_ref.shape[0]
    inside = near_ref.shape[0]
    right = pl.ds(n - REACH, REACH)
    later = [
        pltpu.make_async_copy(nb_hbm.at[pl.ds(0, REACH)], nbo_ref.at[pl.ds(0, REACH)], big.at[0]),
        pltpu.make_async_copy(nb_hbm.at[right], nbo_ref.at[pl.ds(REACH, REACH)], big.at[1]),
        pltpu.make_async_copy(lc_hbm.at[pl.ds(0, REACH)], lco_ref.at[pl.ds(0, REACH)], big.at[2]),
        pltpu.make_async_copy(lc_hbm.at[right], lco_ref.at[pl.ds(REACH, REACH)], big.at[3]),
    ]
    w = c2_ref.shape[1]
    lists = lists_in(near_hbm, count_hbm, far_hbm, ni_ref, nc_ref, fi_ref, small)
    for copy in lists + later:
        copy.start()
    lo = low(w)

    @pl.loop(0, n // 8)
    def _(g):
        for q in range(4):
            k = 4 * g + q
            both_ways(cp_ref[k], c2_ref, 2 * k)
            both_ways(sp_ref[k], s2_ref, 2 * k)

    for k in range(2):
        c2_ref[n + k] = jnp.zeros(c2_ref.shape[1:], BF16)
    base = lax.axis_index("wide") * n
    for copy in lists:
        copy.wait()

    @pl.loop(0, inside // 4)
    def _(g):
        for r in range(4):
            q = 4 * g + r
            i = REACH + q
            live = nc_ref[0, i]
            idx = [jnp.where(k < live, ni_ref[k, i] - base, n) for k in range(slots)]
            near_ref[q] = jnp.transpose(nn(side(lo, c2_ref, idx), rows(nb_ref, q)))
            idx = [fi_ref[k, 0, i] - base for k in range(fars)]
            lf_ref[q] = jnp.transpose(nn(side(lo, s2_ref, idx), rows(lc_ref, q)))

    for copy in later:
        copy.wait()


def outer_kernel(near_hbm, count_hbm, far_hbm, c2_ref, s2_ref, f0_ref, f1_ref, nb_ref, lc_ref,
                 near_ref, lf_ref, ctab, stab, ni_ref, nc_ref, fi_ref, small, big):
    slots, fars = nb_ref.shape[1], lc_ref.shape[1]
    n = c2_ref.shape[0] - 2
    w = c2_ref.shape[1]
    copies = lists_in(near_hbm, count_hbm, far_hbm, ni_ref, nc_ref, fi_ref, small) + [
        pltpu.make_async_copy(c2_ref.at[pl.ds(0, n)], ctab.at[pl.ds(REACH, n)], big.at[0]),
        pltpu.make_async_copy(s2_ref, stab.at[pl.ds(REACH, n)], big.at[1]),
    ]
    for copy in copies:
        copy.start()
    lo = low(w)
    pos = lax.axis_index("wide")
    odd = pos % 2
    half = REACH // 2
    for f_ref, right in ((f0_ref, 1 - odd), (f1_ref, odd)):
        at = right * (n + REACH)
        for k in range(half):
            both_ways(f_ref[k], ctab, at + 2 * k)
            both_ways(f_ref[half + k], stab, at + 2 * k)
    for k in range(2):
        ctab[n + 2 * REACH + k] = jnp.zeros(ctab.shape[1:], BF16)
    base = pos * n - REACH
    for copy in copies:
        copy.wait()

    @pl.loop(0, 2)
    def _(g):
        for q in range(REACH):
            j = g * REACH + q
            i = g * (n - REACH) + q
            live = nc_ref[0, i]
            idx = [jnp.where(k < live, ni_ref[k, i] - base, n + 2 * REACH) for k in range(slots)]
            near_ref[j] = jnp.transpose(nn(side(lo, ctab, idx), rows(nb_ref, j)))
            idx = [fi_ref[k, 0, i] - base for k in range(fars)]
            lf_ref[j] = jnp.transpose(nn(side(lo, stab, idx), rows(lc_ref, j)))


def middle_kernel(mid_hbm, mp_ref, f0_ref, f1_ref, mc_ref, dm_ref, dtop_ref, mf_ref, both_ref, mtab, mi_ref, small):
    mids, mfars = mc_ref.shape[:2]
    w = mtab.shape[1]
    copy = pltpu.make_async_copy(mid_hbm, mi_ref, small.at[0])
    copy.start()
    lo = low(w)
    pos = lax.axis_index("wide")
    odd = pos % 2
    for k in range(mids // 2):
        both_ways(mp_ref[k], mtab, MREACH + 2 * k)
    for f_ref, right in ((f0_ref, 1 - odd), (f1_ref, odd)):
        for k in range(MREACH // 2):
            both_ways(f_ref[REACH + k], mtab, right * (mids + MREACH) + 2 * k)
    both_ref[...] = nn(rows(dm_ref, pl.ds(0, mids)), dtop_ref[0]).astype(BF16)
    base = pos * mids - MREACH
    copy.wait()
    for j in range(mids):
        idx = [mi_ref[j, 0, k] - base for k in range(mfars)]
        mf_ref[j] = jnp.transpose(nn(side(lo, mtab, idx), rows(mc_ref, j)))


def down_kernel(own_ref, over_ref, tc_ref, both_ref, tl_ref, cb_ref, neari_ref, lfi_ref, nearo_ref, lfo_ref, mf_ref,
                out_hbm, out_ref, sems):
    mids = mf_ref.shape[0]
    n = tl_ref.shape[0]
    me = lax.axis_index("narrow")
    acc = None
    for ref, k, h in ((own_ref, 1, me ^ 2), (over_ref, 0, me ^ 1), (over_ref, 1, me ^ 3)):
        part = nn(ref[k], tc_ref[h])
        acc = part if acc is None else acc + part
    down = nt(both_ref[...], acc.astype(BF16))
    r = tl_ref.shape[1]
    copies = []
    for m in range(mids):
        md = (mf_ref[m] + down[m * r : (m + 1) * r]).astype(BF16)
        ld = nn(rows(tl_ref, pl.ds(4 * m, 4)), md)
        for q in range(4):
            i = 4 * m + q
            if REACH <= i < n - REACH:
                near, lf = neari_ref[i - REACH], lfi_ref[i - REACH]
            else:
                j = i if i < REACH else i - (n - 2 * REACH)
                near, lf = nearo_ref[j], lfo_ref[j]
            lq = (lf + ld[q * r : (q + 1) * r]).astype(BF16)
            out_ref[i] = (near + nn(cb_ref[i], lq)).astype(BF16)
        part = pl.ds(4 * m, 4)
        copy = pltpu.make_async_copy(out_ref.at[part], out_hbm.at[part], sems.at[m])
        copy.start()
        copies.append(copy)
    for copy in copies:
        copy.wait()


def apply(
    charges, leaf_row_basis, leaf_column_basis, near_blocks, near_src, near_count, leaf_coupling, far_src,
    up_leaf, column_transfer_leaf, mid_coupling, mid_src, up_mid, down_mid, up_top, down_top, top_coupling,
):
    n, w, v = charges.shape[1:]
    mids = up_mid.shape[1]
    wide, narrow = lax.axis_size("wide"), lax.axis_size("narrow")
    both = ("wide", "narrow")
    pairs = REACH + MREACH // 2
    slots, fars, mfars = near_src.shape[2], far_src.shape[2], mid_src.shape[2]
    hbm = pl.BlockSpec(memory_space=pltpu.HBM)
    vm = pl.BlockSpec(memory_space=pltpu.VMEM)
    dma = pltpu.SemaphoreType.DMA

    def shp(*s, t=BF16):
        return jax.ShapeDtypeStruct(s, t)

    inside = n - 2 * REACH
    cp, sp, mp, e0, e1, term, nbi, lci = pl.pallas_call(
        up_kernel,
        in_specs=[hbm] * 7,
        out_specs=[vm] * 8,
        out_shape=[shp(n // 2, v, 2 * w), shp(n // 2, v, 2 * w), shp(mids // 2, v, 2 * w),
                   shp(pairs, v, 2 * w), shp(pairs, v, 2 * w), shp(v, w),
                   shp(inside, slots, w, v), shp(inside, fars, w, v)],
        scratch_shapes=[
            pltpu.VMEM((n, w, v), BF16), pltpu.VMEM((n, w, v), BF16), pltpu.VMEM((n, w, v), BF16),
            pltpu.VMEM((mids, w, v), BF16), pltpu.VMEM((1, w, v), BF16), dma((7,)),
        ],
        compiler_params=pltpu.CompilerParams(vmem_limit_bytes=16 << 20),
        cost_estimate=pl.CostEstimate(flops=30_000_000, bytes_accessed=4_000_000, transcendentals=0),
        name="up",
    )(*map(in_hbm, (charges[0], leaf_row_basis[0], up_leaf[0], up_mid[0], up_top[0],
                  near_blocks[0], leaf_coupling[0])))

    def xor(x, dw, dn):
        return lax.ppermute(x, both, [(i * narrow + j, (i ^ dw) * narrow + (j ^ dn)) for i in range(wide) for j in range(narrow)])

    f0 = lax.ppermute(e0, "wide", [(i, i ^ 1) for i in range(wide)])
    ends = (0, wide - 1)
    f1 = lax.ppermute(e1, both, [
        (i * narrow + j, i * narrow + (j ^ 1) if i in ends else (((i + 1) ^ 1) - 1) * narrow + j)
        for i in range(wide) for j in range(narrow)
    ])
    f = term.astype(F32)
    own = (f + xor(term, 1, 0).astype(F32)).astype(BF16)
    have = jnp.stack([own, xor(own, 0, 2)])
    bit = 2
    while bit < wide:
        got = have.astype(F32) + xor(have, bit, 0).astype(F32)
        if 2 * bit < wide:
            got = got + xor(have, 2 * bit, 0).astype(F32) + xor(have, 3 * bit, 0).astype(F32)
        have = got.astype(BF16)
        bit *= 4
    over = xor(have, 0, 1)

    near_list = jnp.transpose(near_src, (0, 2, 1))[0]
    far_list = jnp.transpose(far_src, (2, 0, 1))
    mid_list = jnp.transpose(mid_src, (1, 0, 2))
    raw = tuple(map(in_hbm, (near_list, near_count, far_list)))
    near_i, lf_i, c2, s2, nbo, lco = pl.pallas_call(
        inner_kernel,
        in_specs=[hbm] * 3 + [vm] * 4 + [hbm] * 2,
        out_specs=[vm] * 6,
        out_shape=[shp(inside, w, v, t=F32), shp(inside, w, v, t=F32), shp(n + 2, v, 2 * w), shp(n, v, 2 * w),
                   shp(2 * REACH, slots, w, v), shp(2 * REACH, fars, w, v)],
        scratch_shapes=[
            pltpu.SMEM((slots, n), jnp.int32), pltpu.SMEM((1, n), jnp.int32), pltpu.SMEM((fars, 1, n), jnp.int32),
            dma((3,)), dma((4,)),
        ],
        compiler_params=pltpu.CompilerParams(vmem_limit_bytes=12 << 20),
        cost_estimate=pl.CostEstimate(flops=60_000_000, bytes_accessed=6_000_000, transcendentals=0),
        name="inner",
    )(*raw, cp, sp, nbi, lci, in_hbm(near_blocks[0]), in_hbm(leaf_coupling[0]))
    near_o, lf_o = pl.pallas_call(
        outer_kernel,
        in_specs=[hbm] * 3 + [vm] * 6,
        out_specs=[vm] * 2,
        out_shape=[shp(2 * REACH, w, v, t=F32), shp(2 * REACH, w, v, t=F32)],
        scratch_shapes=[
            pltpu.VMEM((n + 2 * REACH + 2, v, 2 * w), BF16),
            pltpu.VMEM((n + 2 * REACH, v, 2 * w), BF16),
            pltpu.SMEM((slots, n), jnp.int32), pltpu.SMEM((1, n), jnp.int32), pltpu.SMEM((fars, 1, n), jnp.int32),
            dma((3,)), dma((4,)),
        ],
        compiler_params=pltpu.CompilerParams(vmem_limit_bytes=16 << 20),
        cost_estimate=pl.CostEstimate(flops=140_000_000, bytes_accessed=8_000_000, transcendentals=0),
        name="outer",
    )(*raw, c2, s2, f0, f1, nbo, lco)
    mf, down_both = pl.pallas_call(
        middle_kernel,
        in_specs=[hbm] + [vm] * 6,
        out_specs=[vm] * 2,
        out_shape=[shp(mids, w, v, t=F32), shp(mids * w, w)],
        scratch_shapes=[
            pltpu.VMEM((mids + 2 * MREACH, v, 2 * w), BF16), pltpu.SMEM((mids, 1, mfars), jnp.int32), dma((1,)),
        ],
        compiler_params=pltpu.CompilerParams(vmem_limit_bytes=8 << 20),
        cost_estimate=pl.CostEstimate(flops=20_000_000, bytes_accessed=3_000_000, transcendentals=0),
        name="middle",
    )(in_hbm(mid_list), mp, f0, f1, mid_coupling[0], down_mid[0], down_top[0])

    out = pl.pallas_call(
        down_kernel,
        in_specs=[vm] * 11,
        out_specs=hbm,
        out_shape=shp(n, w, v),
        scratch_shapes=[pltpu.VMEM((n, w, v), BF16), dma((mids,))],
        compiler_params=pltpu.CompilerParams(vmem_limit_bytes=16 << 20),
        cost_estimate=pl.CostEstimate(flops=30_000_000, bytes_accessed=4_000_000, transcendentals=0),
        name="down",
    )(have, over, top_coupling[0], down_both, column_transfer_leaf[0], leaf_column_basis[0],
      near_i, lf_i, near_o, lf_o, mf)
    return out[None]


def solution(mesh):
    leaf = P("narrow", "wide", None, None)
    block = P("narrow", "wide", None, None, None)
    lists = P("narrow", "wide", None)
    return jax.shard_map(
        apply,
        mesh=mesh,
        in_specs=(
            leaf, leaf, leaf, block, lists, P("narrow", "wide"), block, lists,
            leaf, leaf, block, lists, leaf, leaf, leaf, leaf, P("narrow", None, None, None),
        ),
        out_specs=leaf,
        check_vma=False,
    )
```
